32 devices in a mesh: seq: 8 (over y, x, core), head: 4 (over z).
Axes of the slice: x: 2, y: 2, z: 4, core: 2. Of those that a mesh axis runs over, the one named last changes fastest.
Arguments:
- tokens: bfloat16 [8, 1024, 1024], P('seq', 'head'), may hold values from -6 to 6
- cotangent: bfloat16 [8, 1024, 1024], P('seq', 'head'), may hold values from -6 to 6
- time_embed: bfloat16 [8, 256], P('seq'), may hold values from -6 to 6
- lengths: int32 [8], P('seq'), may hold values from 32 to 1024, as said below
- key_mask: int32 [8, 1024], P('seq'), may hold values from 0 to 1, as said below
- time_weight: bfloat16 [256, 2048], P(('seq', 'head')), may hold values from -0.09375 to 0.09375
- gain_attn: bfloat16 [1024], P(('seq', 'head')), may hold values from 0.5 to 1.5
- qkv_weight: bfloat16 [1024, 3072], P(('seq', 'head')), may hold values from -0.1875 to 0.1875
- out_weight: bfloat16 [1024, 1024], P(('seq', 'head')), may hold values from -1.5 to 1.5
- gain_mlp: bfloat16 [1024], P(('seq', 'head')), may hold values from 0.5 to 1.5
- in_weight: bfloat16 [1024, 4096], P(('seq', 'head')), may hold values from -0.1875 to 0.1875
- down_weight: bfloat16 [4096, 1024], P(('seq', 'head')), may hold values from -0.09375 to 0.09375
Outputs:
- output: bfloat16 [8, 1024, 1024], P('seq', 'head')
- grad_tokens: bfloat16 [8, 1024, 1024], P('seq', 'head')
- grad_time_weight: float32 [256, 2048], P(('seq', 'head'))
- grad_gain_attn: float32 [1024], P(('seq', 'head'))
- grad_qkv_weight: float32 [1024, 3072], P(('seq', 'head'))
- grad_out_weight: float32 [1024, 1024], P(('seq', 'head'))
- grad_gain_mlp: float32 [1024], P(('seq', 'head'))
- grad_in_weight: float32 [1024, 4096], P(('seq', 'head'))
- grad_down_weight: float32 [4096, 1024], P(('seq', 'head'))
The draws below stay inside these ranges and needn't reach their ends.
Inputs may be any that keep to these rules, and one draw needn't show every extreme that they name: `lengths`: the first sequence has 1024 tokens and the last 32. `key_mask`: position 0 of every sequence is 1.
All inputs are finite; a program needn't handle non-finite values.
Results may differ from the reference program's by a relative error of at most 0.015.
Values may be sent and summed in bfloat16 or wider, within the bound.
No kernel may reach another device: no remote copies, remote signals or barrier semaphores. Data moves between devices by JAX's collectives and lax.ppermute only.
A program may use at most 192 MiB of HBM per device.

```python
import math
import jax
import jax.numpy as jnp
from jax import lax

D = 1024
HEADS = 16
HD = 64
FF = 4096
TE = 256
L = 1024
MIN_LEN = 32
SEQ_DEV = 1
SEQS = 8


def draw_lengths(key, part):
    key_one = jax.random.fold_in(key, 11)
    key_two = jax.random.fold_in(key, 12)
    groups = SEQS // SEQ_DEV
    levels = jax.random.randint(key_one, (groups,), 0, 3)
    ceiling = jnp.where(levels == 0, L, jnp.where(levels == 1, L // 2, L // 8))
    ceiling = jnp.maximum(ceiling, MIN_LEN)
    ceiling = jnp.repeat(ceiling, SEQ_DEV)
    floor_len = jnp.maximum(ceiling // 2, MIN_LEN)
    drawn = jax.random.randint(key_two, (SEQS,), floor_len, ceiling + 1)
    drawn = drawn.at[0].set(L).at[SEQS - 1].set(MIN_LEN)
    return drawn.astype(jnp.int32)


def draw_key_mask(key, part):
    values = jax.random.randint(jax.random.fold_in(key, 21), (SEQS, L), 0, 8)
    kept_mask = (values > 0).astype(jnp.int32)
    return kept_mask.at[:, 0].set(1)


def shard_levels(own_key, extent, cuts, low, largest):
    def one(axis_at, blocks):
        draws = jax.random.uniform(jax.random.fold_in(jax.random.fold_in(own_key, 6), axis_at), (blocks,), jnp.float32, low / len(cuts), largest / len(cuts))
        return jnp.repeat(jnp.exp(draws), extent[axis_at] // blocks).reshape((-1,) + (1,) * (len(extent) - axis_at - 1))

    loudness = one(*cuts[0])
    for cut in cuts[1:]:
        loudness = loudness * one(*cut)
    return loudness


def gaussian(rng, dims, deviation, reach, shards=(), held_as=jnp.bfloat16):
    factor_of = shard_levels(rng, dims, shards, -0.22, 0.18) if shards else 1.0
    values = jax.random.normal(rng, dims, jnp.float32) * deviation * factor_of
    return jnp.minimum(jnp.maximum(values, -reach), reach).astype(held_as)


def setup_inputs(seed: int = 0) -> dict:
    splits = jax.random.split(jax.random.key(seed), 13)
    return {
        "tokens": gaussian(splits[0], (SEQS, L, D), 1.0, 6.0, ((0, 8), (1, 4))),
        "cotangent": gaussian(splits[1], (SEQS, L, D), 1.0, 6.0, ((0, 8), (1, 4))),
        "time_embed": gaussian(splits[2], (SEQS, TE), 1.0, 6.0, ((0, 8),)),
        "lengths": draw_lengths(jax.random.fold_in(splits[12], 71), 0),
        "key_mask": draw_key_mask(jax.random.fold_in(splits[12], 71), 0),
        "time_weight": gaussian(splits[5], (TE, 2 * D), (16 * TE) ** -0.5, 0.09375, ((0, 32),)),
        "gain_attn": jnp.clip(1.0 + 0.1 * jax.random.normal(splits[6], (D,), jnp.float32), 0.5, 1.5).astype(jnp.bfloat16),
        "qkv_weight": gaussian(splits[7], (D, 3 * D), D ** -0.5, 0.1875, ((0, 32),)),
        "out_weight": gaussian(splits[8], (D, D), (D // 64) ** -0.5, 1.5, ((0, 32),)),
        "gain_mlp": jnp.clip(1.0 + 0.1 * jax.random.normal(splits[9], (D,), jnp.float32), 0.5, 1.5).astype(jnp.bfloat16),
        "in_weight": gaussian(splits[10], (D, FF), D ** -0.5, 0.1875, ((0, 32),)),
        "down_weight": gaussian(splits[11], (FF, D), FF ** -0.5, 0.09375, ((0, 32),)),
    }


precise = lax.Precision.HIGHEST
epsilon = 1e-05

@jax.custom_vjp
def low(v):
    return lax.optimization_barrier(v.astype(jnp.bfloat16)).astype(jnp.float32)

@jax.custom_vjp
def low_back(v):
    return v

def low_keep(v):
    return (low(v), None)

def low_pass(kept, grad):
    return (grad,)

def back_keep(v):
    return (v, None)

def back_low(kept, grad):
    return (low(grad),)
low.defvjp(low_keep, low_pass)
low_back.defvjp(back_keep, back_low)

def layer_norm(field_in, gain_vec, scale_vec):
    centre = lax.optimization_barrier(jnp.mean(field_in, axis=-1, keepdims=True))
    shifted = field_in - centre
    variance = lax.optimization_barrier(jnp.mean(shifted * shifted, axis=-1, keepdims=True))
    return shifted * lax.rsqrt(variance + epsilon) * gain_vec * scale_vec

def rope_tables(positions, head_dim):
    half_dim = head_dim // 2
    inverse_freq = jnp.power(10000.0, -jnp.arange(half_dim, dtype=jnp.float32) * 2.0 / head_dim)
    angles = positions.astype(jnp.float32)[:, None] * inverse_freq[None, :]
    return (jnp.cos(angles)[:, None, :], jnp.sin(angles)[:, None, :])

def rotate(field_in, cosine_table, sine_table):
    half_dim = field_in.shape[-1] // 2
    first_half = field_in[..., :half_dim]
    second_half = field_in[..., half_dim:]
    return jnp.concatenate([first_half * cosine_table - second_half * sine_table, second_half * cosine_table + first_half * sine_table], axis=-1)

def attend_one(inputs):
    query_rows, key_all, value_all, key_ok = inputs
    length = query_rows.shape[0]
    block_rows = min(512, length)
    scale_val = 1.0 / math.sqrt(query_rows.shape[-1])
    blocks_out = []
    for row_start in range(0, length, block_rows):
        scores = jnp.einsum('qhd,khd->hqk', query_rows[row_start:row_start + block_rows], key_all, precision=precise) * scale_val
        scores = jnp.where(key_ok[None, None, :], scores, -1e+30)
        scores = low_back(scores)
        row_max = lax.optimization_barrier(jnp.max(scores, axis=-1, keepdims=True))
        weights = jnp.exp(scores - row_max)
        probabilities = low(weights / lax.optimization_barrier(jnp.sum(weights, axis=-1, keepdims=True)))
        blocks_out.append(jnp.einsum('hqk,khd->qhd', probabilities, value_all, precision=precise))
    return jnp.concatenate(blocks_out, axis=0)

def forward(tokens, embed_part, key_ok, valid_rows, time_weight, gain_attn, qkv_weight, out_weight, gain_mlp, in_weight, down_weight):
    group_size = tokens.shape[0]
    positions = jnp.arange(L, dtype=jnp.int32)
    cosine_table, sine_table = rope_tables(positions, HD)
    scales = jnp.dot(embed_part, time_weight, precision=precise)
    normed = low(layer_norm(tokens, gain_attn, 1.0 + scales[:, None, :D]))
    packed = low_back(jnp.einsum('gld,de->gle', normed, qkv_weight, precision=precise))
    packed = packed.reshape(group_size, L, 3, HEADS, HD)
    queries = low_back(low(rotate(packed[:, :, 0], cosine_table, sine_table)))
    keys_rot = low_back(low(rotate(packed[:, :, 1], cosine_table, sine_table)))
    values = low_back(low(packed[:, :, 2]))
    mixed_heads = lax.map(jax.checkpoint(attend_one), (queries, keys_rot, values, key_ok))
    mixed_heads = low_back(low(mixed_heads)).reshape(group_size, L, D)
    attn_out = low_back(jnp.einsum('gld,de->gle', mixed_heads, out_weight, precision=precise))
    hidden = tokens + valid_rows[..., None] * attn_out
    normed_mlp = low(layer_norm(hidden, gain_mlp, 1.0 + scales[:, None, D:]))
    upper_proj = low_back(jnp.einsum('gld,df->glf', normed_mlp, in_weight, precision=precise))
    activation = low(0.5 * upper_proj * (1.0 + lax.erf(upper_proj / math.sqrt(2.0))))
    mlp_out = low_back(jnp.einsum('glf,fd->gld', activation, down_weight, precision=precise))
    return hidden + valid_rows[..., None] * mlp_out

def reference(tokens, cotangent, time_embed, lengths, key_mask, time_weight, gain_attn, qkv_weight, out_weight, gain_mlp, in_weight, down_weight):
    group_size = math.gcd(SEQS, max(1, 4096 // L))
    step_count = SEQS // group_size
    weight_list = tuple((w.astype(jnp.float32) for w in (time_weight, gain_attn, qkv_weight, out_weight, gain_mlp, in_weight, down_weight)))
    positions = jnp.arange(L, dtype=jnp.int32)

    def one_group(totals, pieces):
        tok_part, cot_part, embed_part, length_part, mask_part = pieces
        inside = positions[None, :] < length_part[:, None]
        valid_rows = inside.astype(jnp.float32)
        key_ok = jnp.logical_and(mask_part > 0, inside)

        def forward_group(tok_float, *weight_args):
            return forward(tok_float, embed_part.astype(jnp.float32), key_ok, valid_rows, *weight_args)
        result, pullback = jax.vjp(forward_group, tok_part.astype(jnp.float32), *weight_list)
        gradients = pullback(cot_part.astype(jnp.float32))
        totals = tuple((total + grad for total, grad in zip(totals, gradients[1:])))
        return (totals, (result.astype(jnp.bfloat16), gradients[0].astype(jnp.bfloat16)))
    pieces = (tokens.reshape(step_count, group_size, L, D), cotangent.reshape(step_count, group_size, L, D), time_embed.reshape(step_count, group_size, TE), lengths.reshape(step_count, group_size), key_mask.reshape(step_count, group_size, L))
    zero_grads = tuple((jnp.zeros(w.shape, jnp.float32) for w in weight_list))
    totals, (outputs, grad_rows) = lax.scan(one_group, zero_grads, pieces)
    return (outputs.reshape(SEQS, L, D), grad_rows.reshape(SEQS, L, D), totals[0], totals[1], totals[2], totals[3], totals[4], totals[5], totals[6])
```

```python
import math

import jax
import jax.numpy as jnp
from jax import lax
from jax.sharding import PartitionSpec as P

HEADS = 16
HD = 64

epsilon = 1e-05
f32 = jnp.float32
bf16 = jnp.bfloat16


def dot(left, right):
    return jnp.dot(left, right, preferred_element_type=f32)


def dot_right_t(left, right):
    return lax.dot_general(left, right, (((1,), (1,)), ((), ())), preferred_element_type=f32)


def dot_left_t(left, right):
    return lax.dot_general(left, right, (((0,), (0,)), ((), ())), preferred_element_type=f32)


def whiten(field):
    centre = jnp.mean(field, axis=-1, keepdims=True)
    shifted = field - centre
    variance = jnp.mean(shifted * shifted, axis=-1, keepdims=True)
    inv_std = lax.rsqrt(variance + epsilon)
    return shifted * inv_std, inv_std


def whiten_back(d_normed, whitened, inv_std, scale_vec):
    d_scale = jnp.sum(d_normed * whitened, axis=0, keepdims=True)
    d_white = d_normed * scale_vec
    d_input = inv_std * (
        d_white
        - jnp.mean(d_white, axis=-1, keepdims=True)
        - whitened * jnp.mean(d_white * whitened, axis=-1, keepdims=True)
    )
    return d_input, d_scale


def rope_tables(positions, repeats):
    half_dim = HD // 2
    inverse_freq = jnp.power(10000.0, -jnp.arange(half_dim, dtype=f32) * 2.0 / HD)
    angles = positions.astype(f32)[:, None] * inverse_freq[None, :]
    return jnp.cos(angles)[:, None, :], jnp.sin(angles)[:, None, :]


def rotate(field, cosine, sine):
    rows, width = field.shape
    field = field.reshape(rows, width // HD, HD)
    half_dim = HD // 2
    first, second = field[..., :half_dim], field[..., half_dim:]
    turned = jnp.concatenate(
        [first * cosine - second * sine, second * cosine + first * sine], axis=-1
    )
    return turned.reshape(rows, width)


def attend_forward(query, key, value, bias):
    length = query.shape[0]
    block = min(512, length)
    scale = 1.0 / math.sqrt(HD)
    mixed, logs = [], []
    for at in range(0, length, block):
        scores = jnp.einsum("qhd,khd->hqk", query[at : at + block], key, preferred_element_type=f32)
        scores = jnp.where(bias[None, None, :], scores * scale, -1e30)
        row_max = jnp.max(scores, axis=-1, keepdims=True)
        weights = jnp.exp(scores - row_max)
        row_sum = jnp.sum(weights, axis=-1, keepdims=True)
        low = (weights / row_sum).astype(bf16)
        mixed.append(
            jnp.einsum("hqk,khd->qhd", low, value, preferred_element_type=f32).astype(bf16)
        )
        logs.append((row_max + jnp.log(row_sum))[..., 0])
    return jnp.concatenate(mixed, axis=0), jnp.concatenate(logs, axis=1)


def attend_backward(query, key, value, log_sum, d_out, bias):
    length = query.shape[0]
    block = min(512, length)
    scale = 1.0 / math.sqrt(HD)
    d_key = jnp.zeros(key.shape, f32)
    d_value = jnp.zeros(value.shape, f32)
    d_query = []
    for at in range(0, length, block):
        q_block, d_block = query[at : at + block], d_out[at : at + block]
        scores = jnp.einsum("qhd,khd->hqk", q_block, key, preferred_element_type=f32) * scale
        scores = jnp.where(bias[None, None, :], scores, -1e30)
        probs = jnp.exp(scores - log_sum[:, at : at + block, None])
        low = probs.astype(bf16)
        d_value = d_value + jnp.einsum("hqk,qhd->khd", low, d_block, preferred_element_type=f32)
        d_probs = jnp.einsum("qhd,khd->hqk", d_block, value, preferred_element_type=f32)
        row_dot = jnp.sum(d_probs * probs, axis=-1, keepdims=True)
        d_scores = (probs * (d_probs - row_dot)).astype(bf16)
        d_query.append(
            jnp.einsum("hqk,khd->qhd", d_scores, key, preferred_element_type=f32) * scale
        )
        d_key = d_key + scale * jnp.einsum(
            "hqk,qhd->khd", d_scores, q_block, preferred_element_type=f32
        )
    return jnp.concatenate(d_query, axis=0), d_key, d_value


def build(seq_size, head_size):
    plane_bits = (seq_size // 2).bit_length() - 1
    planes = seq_size // 2
    assert planes == 1 << plane_bits and seq_size >= 2 and head_size == 4

    core_pairs = [(i, i ^ 1) for i in range(seq_size)]
    swap_pairs = [
        (s * head_size + h, (s ^ 1) * head_size + (h ^ 2))
        for s in range(seq_size)
        for h in range(head_size)
        if (s & 1) != (h >> 1)
    ]

    def over_core(x):
        return lax.ppermute(x, "seq", core_pairs)

    def over_plane(x, bit):
        return lax.ppermute(x, "seq", [(i, i ^ (2 << bit)) for i in range(seq_size)])

    def over_z(x, mask):
        return lax.ppermute(x, "head", [(i, i ^ mask) for i in range(head_size)])

    def pick(x, index, axis):
        return lax.dynamic_index_in_dim(x, index, axis, keepdims=False)

    def join(own, other, bit, axis=0):
        return jnp.where(
            bit == 0, jnp.stack([own, other], axis=axis), jnp.stack([other, own], axis=axis)
        )

    def per_device(
        tokens,
        cotangent,
        time_embed,
        lengths,
        key_mask,
        time_weight,
        gain_attn,
        qkv_weight,
        out_weight,
        gain_mlp,
        in_weight,
        down_weight,
    ):
        seq_at, z = lax.axis_index("seq"), lax.axis_index("head")
        core, plane = seq_at & 1, seq_at >> 1
        group, side = z >> 1, z & 1
        stays = core == group
        _, span, width = tokens.shape
        full_len = span * head_size
        half_width = width // 2
        hidden_cols = in_weight.shape[1]
        half_hidden = hidden_cols // 2
        orders = (tuple(range(plane_bits)), tuple(reversed(range(plane_bits))))

        def moved(x):
            return jnp.where(stays, x, lax.ppermute(x, ("seq", "head"), swap_pairs))

        def gather(x, order, paired):
            y = join(x, over_z(x, 2), z >> 1)
            y = join(y, over_z(y, 1), z & 1)
            for bit in order:
                y = join(y, over_plane(y, bit), (plane >> bit) & 1)
            n = plane_bits
            at = [list(reversed(order)).index(b) for b in reversed(range(n))]
            tail = [n, n + 1]
            rest = list(range(n + 2, y.ndim))
            if paired:
                perm = at + [rest[0]] + [tail[1], tail[0]] + rest[1:]
            else:
                perm = at + [tail[1], tail[0]] + rest
            y = y.transpose(perm)
            return y.reshape(-1, x.shape[-1])

        def reduce_rows(x, order, paired):
            cols = x.shape[-1]
            y = x.astype(bf16).reshape(
                (2,) * plane_bits + ((2,) if paired else ()) + (2, 2, -1, cols)
            )
            alive = list(reversed(range(plane_bits)))
            for bit in order:
                axis = alive.index(bit)
                mine = (plane >> bit) & 1
                other = over_plane(pick(y, 1 - mine, axis), bit)
                y = (pick(y, mine, axis).astype(f32) + other.astype(f32)).astype(bf16)
                alive.remove(bit)
            axis = 1 if paired else 0
            mine = z & 1
            other = over_z(pick(y, 1 - mine, axis + 1), 1)
            y = (pick(y, mine, axis + 1).astype(f32) + other.astype(f32)).astype(bf16)
            mine = z >> 1
            other = over_z(pick(y, 1 - mine, axis), 2)
            return pick(y, mine, axis).astype(f32) + other.astype(f32)

        chunk = out_weight.shape[0] * head_size
        aligned = chunk % HD == 0
        head_chunk = chunk if aligned else half_width

        def qkv_half(w, which):
            rows = w.shape[0]
            w = w.reshape(rows, 3, -1, 2, head_chunk)
            w = pick(w, which, 3).reshape(rows, 3, 2, half_width // 2)
            return w.transpose(0, 2, 1, 3).reshape(rows, 3 * half_width)

        def qkv_whole(own, other):
            rows = own.shape[0]

            def back(v):
                v = v.reshape(rows, 2, 3, half_width // 2).transpose(0, 2, 1, 3)
                return v.reshape(rows, 3, -1, head_chunk)

            return join(back(own), back(other), core, 3).reshape(rows, 3 * width)

        hidden_chunk = down_weight.shape[0] * head_size

        def in_half(w, which):
            rows = w.shape[0]
            return pick(w.reshape(rows, -1, 2, hidden_chunk), which, 2).reshape(rows, half_hidden)

        def in_whole(own, other):
            rows = own.shape[0]
            shape = (rows, -1, hidden_chunk)
            return join(own.reshape(shape), other.reshape(shape), core, 2).reshape(
                rows, hidden_cols
            )

        aux = jnp.concatenate(
            [
                key_mask.astype(f32),
                time_embed.astype(f32),
                jnp.broadcast_to(lengths.astype(f32)[:, None], (1, 128)),
            ],
            axis=1,
        )
        aux_other = over_core(aux)
        aux_both = join(aux[0], aux_other[0], core)
        embed_both = aux_both[:, full_len : full_len + time_embed.shape[1]]
        aux_mine = pick(aux_both, group, 0)
        length = aux_mine[full_len + time_embed.shape[1]].astype(jnp.int32)
        usable = jnp.logical_and(
            aux_mine[:full_len] > 0, jnp.arange(full_len, dtype=jnp.int32) < length
        )

        qkv_scaled = (qkv_weight.astype(f32) * gain_attn.astype(f32)[:, None]).astype(bf16)
        in_scaled = (in_weight.astype(f32) * gain_mlp.astype(f32)[:, None]).astype(bf16)
        qkv_pair = join(
            qkv_half(qkv_scaled, core), over_core(qkv_half(qkv_scaled, 1 - core)), core
        )
        in_pair = join(in_half(in_scaled, core), over_core(in_half(in_scaled, 1 - core)), core)
        cut = 3 * half_width // 2
        w_qkv = jnp.concatenate(
            [
                gather(qkv_pair[..., :cut], orders[0], True),
                gather(qkv_pair[..., cut:], orders[1], True),
            ],
            axis=1,
        )
        if aligned:
            w_out = gather(out_weight, orders[0], False)
        else:
            out_pair = join(out_weight, over_core(out_weight), core)
            w_out = lax.dynamic_slice_in_dim(
                gather(out_pair, orders[0], True), core * half_width, half_width, 0
            )
        w_in = gather(in_pair, orders[1], True)
        w_down = gather(down_weight, orders[0], False)

        t_rows = time_weight
        for bit in orders[0]:
            t_rows = join(t_rows, over_plane(t_rows, bit), (plane >> bit) & 1)
        t_rows = t_rows.reshape(-1, 2 * width)
        embed_rows = pick(
            pick(embed_both.reshape(2, planes, 2, head_size, -1), core, 2), z, 2
        ).reshape(2, -1)
        part = jnp.dot(
            embed_rows, t_rows.astype(f32), precision=lax.Precision.HIGHEST
        )
        part_mine = pick(part, group, 0) + over_z(pick(part, 1 - group, 0), 2)
        part_mine = part_mine + over_z(part_mine, 1)
        scales = 1.0 + (part_mine + over_core(part_mine))
        scale_attn, scale_mlp = scales[None, :width], scales[None, width:]

        own_block = side + 2 * core
        positions = own_block * span + jnp.arange(span, dtype=jnp.int32)
        other_positions = (side + 2 - 2 * core) * span + jnp.arange(span, dtype=jnp.int32)
        valid = (positions < length).astype(f32)[:, None]
        chip_positions = jnp.concatenate([positions, other_positions])
        cosine, sine = rope_tables(chip_positions, 0)
        usable_blocks = usable.reshape(head_size, span)
        bias = jnp.concatenate(
            [
                pick(usable_blocks, block, 0)
                for block in (
                    side + 2 * core,
                    side + 2 - 2 * core,
                    1 - side + 2 * core,
                    1 - side + 2 - 2 * core,
                )
            ]
        )

        inputs = moved(tokens[0]).astype(f32)
        upstream = moved(cotangent[0]).astype(f32)
        white_a, inv_a = whiten(inputs)
        normed_a = (white_a * scale_attn).astype(bf16)
        chip_a = jnp.concatenate([normed_a, over_core(normed_a)])
        packed = dot(chip_a, w_qkv).reshape(2 * span, 2, 3, half_width // 2)

        def ready(which):
            three = pick(packed, which, 1)
            return jnp.concatenate(
                [
                    rotate(three[:, 0], cosine, sine).astype(bf16),
                    rotate(three[:, 1], cosine, sine).astype(bf16),
                    three[:, 2].astype(bf16),
                ],
                axis=1,
            )

        qkv_all = jnp.concatenate([ready(side), over_z(ready(1 - side), 1)])
        quarter = half_width // 2
        head_shape = (full_len, quarter // HD, HD)
        query = qkv_all[:, :quarter].reshape(head_shape)
        key = qkv_all[:, quarter : 2 * quarter].reshape(head_shape)
        value = qkv_all[:, 2 * quarter :].reshape(head_shape)
        mixed_heads, log_sum = attend_forward(query, key, value, bias)
        mixed_heads = mixed_heads.reshape(full_len, quarter)
        chip_len = 2 * span
        mixed = join(
            mixed_heads[:chip_len], over_z(mixed_heads[chip_len:], 1), side, 1
        ).reshape(chip_len, half_width)

        def pair_sum(x):
            return x[:span] + over_core(x[span:].astype(bf16)).astype(f32)

        hidden = inputs + valid * pair_sum(dot(mixed, w_out))
        white_m, inv_m = whiten(hidden)
        normed_m = (white_m * scale_mlp).astype(bf16)
        chip_m = jnp.concatenate([normed_m, over_core(normed_m)])
        upper = dot(chip_m, w_in)
        phi = 0.5 * (1.0 + lax.erf(upper / math.sqrt(2.0)))
        activation = (upper * phi).astype(bf16)
        slope = phi + upper * jnp.exp(-0.5 * upper * upper) / math.sqrt(2.0 * math.pi)
        output = hidden + valid * pair_sum(dot(activation, w_down))
        output = moved(output.astype(bf16))[None]

        d_mlp = (valid * upstream).astype(bf16)
        chip_d = jnp.concatenate([d_mlp, over_core(d_mlp)])
        d_upper = (dot_right_t(chip_d, w_down) * slope).astype(bf16)
        sum_down = reduce_rows(dot_left_t(activation, chip_d), orders[0], False)
        d_normed_m = pair_sum(dot_right_t(d_upper, w_in))
        sum_in_half = reduce_rows(dot_left_t(chip_m, d_upper), orders[1], True)
        d_from_m, d_scale_m = whiten_back(d_normed_m, white_m, inv_m, scale_mlp)
        d_hidden = upstream + d_from_m
        d_attn = (valid * d_hidden).astype(bf16)
        chip_da = jnp.concatenate([d_attn, over_core(d_attn)])
        grad_out = dot_left_t(mixed, chip_da)
        if aligned:
            sum_out = reduce_rows(grad_out, orders[0], False)
        else:
            padded = jnp.where(
                core == 0,
                jnp.concatenate([grad_out, jnp.zeros_like(grad_out)]),
                jnp.concatenate([jnp.zeros_like(grad_out), grad_out]),
            )
            out_half = reduce_rows(padded, orders[0], True)
            sum_out = pick(out_half, core, 0) + over_core(pick(out_half, 1 - core, 0))
        d_mixed = dot_right_t(chip_da, w_out).astype(bf16).reshape(chip_len, 2, quarter)
        d_mixed_all = jnp.concatenate(
            [pick(d_mixed, side, 1), over_z(pick(d_mixed, 1 - side, 1), 1)]
        ).reshape(head_shape)
        d_query, d_key, d_value = attend_backward(
            query, key, value, log_sum, d_mixed_all, bias
        )
        d_all = jnp.concatenate(
            [
                x.astype(bf16).reshape(full_len, quarter) for x in (d_query, d_key, d_value)
            ],
            axis=1,
        )
        d_chip = join(d_all[:chip_len], over_z(d_all[chip_len:], 1), side, 1).reshape(
            chip_len, 2, 3, quarter
        )
        d_packed = jnp.stack(
            [
                rotate(d_chip[:, s, k].astype(f32), cosine, -sine).astype(bf16)
                if k < 2
                else d_chip[:, s, k]
                for s in range(2)
                for k in range(3)
            ],
            axis=1,
        ).reshape(chip_len, 3 * half_width)
        grad_qkv = dot_left_t(chip_a, d_packed)
        qkv_sum = jnp.concatenate(
            [
                reduce_rows(grad_qkv[:, :cut], orders[0], True),
                reduce_rows(grad_qkv[:, cut:], orders[1], True),
            ],
            axis=-1,
        )
        d_normed_a = pair_sum(dot_right_t(d_packed, w_qkv))
        d_from_a, d_scale_a = whiten_back(d_normed_a, white_a, inv_a, scale_attn)
        grad_tokens = moved((d_hidden + d_from_a).astype(bf16))[None]

        def across(x):
            return over_core(pick(x, 1 - core, 0).astype(bf16)).astype(f32)

        raw_qkv = qkv_whole(pick(qkv_sum, core, 0), across(qkv_sum))
        raw_in = in_whole(pick(sum_in_half, core, 0), across(sum_in_half))
        sum_gain_a = jnp.sum(raw_qkv * qkv_weight.astype(f32), axis=1)
        sum_gain_m = jnp.sum(raw_in * in_weight.astype(f32), axis=1)
        sum_qkv = raw_qkv * gain_attn.astype(f32)[:, None]
        sum_in = raw_in * gain_mlp.astype(f32)[:, None]

        d_scale = jnp.concatenate([d_scale_a, d_scale_m], axis=1)
        d_scale = d_scale + over_core(d_scale)
        d_scale = d_scale + over_z(d_scale, 1)
        d_both = join(d_scale[0], over_z(d_scale, 2)[0], group)
        rows_time = lax.dot_general(
            embed_rows,
            d_both,
            (((0,), (0,)), ((), ())),
            precision=lax.Precision.HIGHEST,
            preferred_element_type=f32,
        ).reshape((2,) * plane_bits + (-1, 2 * width))
        alive = list(reversed(range(plane_bits)))
        for bit in orders[1]:
            axis = alive.index(bit)
            mine = (plane >> bit) & 1
            rows_time = pick(rows_time, mine, axis) + over_plane(
                pick(rows_time, 1 - mine, axis), bit
            )
            alive.remove(bit)
        return (
            output,
            grad_tokens,
            rows_time,
            sum_gain_a,
            sum_qkv,
            sum_out,
            sum_gain_m,
            sum_in,
            sum_down,
        )

    return per_device


def solution(mesh):
    rows, both, flat = P(("seq", "head"), None), P("seq", "head", None), P(("seq", "head"))
    return jax.shard_map(
        build(mesh.shape["seq"], mesh.shape["head"]),
        mesh=mesh,
        in_specs=(both, both, P("seq", None), P("seq"), P("seq", None), rows, flat, rows, rows, flat, rows, rows),
        out_specs=(both, both, rows, flat, rows, rows, flat, rows, rows),
        check_vma=False,
    )
```

```python
import math

import jax
import jax.numpy as jnp
from jax import lax
from jax.sharding import PartitionSpec as P

HEADS = 16
HD = 64

epsilon = 1e-05
f32 = jnp.float32
bf16 = jnp.bfloat16


def dot(left, right):
    return jnp.dot(left, right, preferred_element_type=f32)


def dot_right_t(left, right):
    return lax.dot_general(left, right, (((1,), (1,)), ((), ())), preferred_element_type=f32)


def dot_left_t(left, right):
    return lax.dot_general(left, right, (((0,), (0,)), ((), ())), preferred_element_type=f32)


def whiten(field):
    centre = jnp.mean(field, axis=-1, keepdims=True)
    shifted = field - centre
    variance = jnp.mean(shifted * shifted, axis=-1, keepdims=True)
    inv_std = lax.rsqrt(variance + epsilon)
    return shifted * inv_std, inv_std


def whiten_back(d_normed, whitened, inv_std, scale_vec):
    d_scale = jnp.sum(d_normed * whitened, axis=0, keepdims=True)
    d_white = d_normed * scale_vec
    d_input = inv_std * (
        d_white
        - jnp.mean(d_white, axis=-1, keepdims=True)
        - whitened * jnp.mean(d_white * whitened, axis=-1, keepdims=True)
    )
    return d_input, d_scale


def rope_tables(positions, repeats):
    half_dim = HD // 2
    inverse_freq = jnp.power(10000.0, -jnp.arange(half_dim, dtype=f32) * 2.0 / HD)
    angles = positions.astype(f32)[:, None] * inverse_freq[None, :]
    return jnp.cos(angles)[:, None, :], jnp.sin(angles)[:, None, :]


def rotate(field, cosine, sine):
    rows, width = field.shape
    field = field.reshape(rows, width // HD, HD)
    half_dim = HD // 2
    first, second = field[..., :half_dim], field[..., half_dim:]
    turned = jnp.concatenate(
        [first * cosine - second * sine, second * cosine + first * sine], axis=-1
    )
    return turned.reshape(rows, width)


def attend_forward(query, key, value, bias):
    length = query.shape[0]
    block = min(512, length)
    scale = 1.0 / math.sqrt(HD)
    mixed, logs = [], []
    for at in range(0, length, block):
        scores = jnp.einsum("qhd,khd->hqk", query[at : at + block], key, preferred_element_type=f32)
        scores = jnp.where(bias[None, None, :], scores * scale, -1e30)
        row_max = jnp.max(scores, axis=-1, keepdims=True)
        weights = jnp.exp(scores - row_max)
        row_sum = jnp.sum(weights, axis=-1, keepdims=True)
        low = (weights / row_sum).astype(bf16)
        mixed.append(
            jnp.einsum("hqk,khd->qhd", low, value, preferred_element_type=f32).astype(bf16)
        )
        logs.append((row_max + jnp.log(row_sum))[..., 0])
    return jnp.concatenate(mixed, axis=0), jnp.concatenate(logs, axis=1)


def attend_backward(query, key, value, log_sum, d_out, bias):
    length = query.shape[0]
    block = min(512, length)
    scale = 1.0 / math.sqrt(HD)
    d_key = jnp.zeros(key.shape, f32)
    d_value = jnp.zeros(value.shape, f32)
    d_query = []
    for at in range(0, length, block):
        q_block, d_block = query[at : at + block], d_out[at : at + block]
        scores = jnp.einsum("qhd,khd->hqk", q_block, key, preferred_element_type=f32) * scale
        scores = jnp.where(bias[None, None, :], scores, -1e30)
        probs = jnp.exp(scores - log_sum[:, at : at + block, None])
        low = probs.astype(bf16)
        d_value = d_value + jnp.einsum("hqk,qhd->khd", low, d_block, preferred_element_type=f32)
        d_probs = jnp.einsum("qhd,khd->hqk", d_block, value, preferred_element_type=f32)
        row_dot = jnp.sum(d_probs * probs, axis=-1, keepdims=True)
        d_scores = (probs * (d_probs - row_dot)).astype(bf16)
        d_query.append(
            jnp.einsum("hqk,khd->qhd", d_scores, key, preferred_element_type=f32) * scale
        )
        d_key = d_key + scale * jnp.einsum(
            "hqk,qhd->khd", d_scores, q_block, preferred_element_type=f32
        )
    return jnp.concatenate(d_query, axis=0), d_key, d_value


def build(seq_size, head_size):
    plane_bits = (seq_size // 2).bit_length() - 1
    planes = seq_size // 2
    assert planes == 1 << plane_bits and seq_size >= 2 and head_size == 4

    core_pairs = [(i, i ^ 1) for i in range(seq_size)]
    swap_pairs = [
        (s * head_size + h, (s ^ 1) * head_size + (h ^ 2))
        for s in range(seq_size)
        for h in range(head_size)
        if (s & 1) != (h >> 1)
    ]

    def over_core(x):
        return lax.ppermute(x, "seq", core_pairs)

    def over_plane(x, bit):
        return lax.ppermute(x, "seq", [(i, i ^ (2 << bit)) for i in range(seq_size)])

    def over_z(x, mask):
        return lax.ppermute(x, "head", [(i, i ^ mask) for i in range(head_size)])

    def pick(x, index, axis):
        return lax.dynamic_index_in_dim(x, index, axis, keepdims=False)

    def join(own, other, bit, axis=0):
        return jnp.where(
            bit == 0, jnp.stack([own, other], axis=axis), jnp.stack([other, own], axis=axis)
        )

    def per_device(
        tokens,
        cotangent,
        time_embed,
        lengths,
        key_mask,
        time_weight,
        gain_attn,
        qkv_weight,
        out_weight,
        gain_mlp,
        in_weight,
        down_weight,
    ):
        seq_at, z = lax.axis_index("seq"), lax.axis_index("head")
        core, plane = seq_at & 1, seq_at >> 1
        group, side = z >> 1, z & 1
        stays = core == group
        _, span, width = tokens.shape
        full_len = span * head_size
        hidden_cols = in_weight.shape[1]
        head_cols, ff_cols = width // 4, hidden_cols // 4
        forwards = tuple(range(plane_bits))
        backwards = tuple(reversed(forwards))
        where = {"c": core, "g": group, "t": side}
        where.update({bit: (plane >> bit) & 1 for bit in range(plane_bits)})
        natural = list(backwards) + ["c", "g", "t"]

        def send(x, axis):
            if axis == "c":
                return over_core(x)
            if axis == "g":
                return over_z(x, 2)
            if axis == "t":
                return over_z(x, 1)
            return over_plane(x, axis)

        def moved(x):
            return jnp.where(stays, x, lax.ppermute(x, ("seq", "head"), swap_pairs))

        def after(x, first):
            return lax.optimization_barrier((x, first))[0]

        def gather(x, labels, axes):
            for axis in axes:
                x = join(x, send(x, axis), where[axis])
                labels = [axis] + labels
            return x, labels

        def in_order(x, labels):
            wanted = [axis for axis in natural if axis in labels]
            perm = [labels.index(axis) for axis in wanted]
            x = x.transpose(perm + list(range(len(perm), x.ndim)))
            return x.reshape(-1, x.shape[-1])

        def exchange(parts, axis):
            mine = where[axis]
            return join(pick(parts, mine, 0), send(pick(parts, 1 - mine, 0), axis), mine)

        def reduce_rows(x, labels, axes):
            labels = [axis for axis in natural if axis in labels]
            y = x.astype(bf16).reshape((2,) * len(labels) + (-1, x.shape[-1]))
            for step, axis in enumerate(axes):
                at, mine = labels.index(axis), where[axis]
                other = send(pick(y, 1 - mine, at), axis)
                y = pick(y, mine, at).astype(f32) + other.astype(f32)
                if step + 1 < len(axes):
                    y = y.astype(bf16)
                labels.remove(axis)
            return y

        chunk = out_weight.shape[0] * head_size
        aligned = (chunk % HD == 0) and (width // (2 * chunk)) % 2 == 0

        def qkv_split(w):
            rows = w.shape[0]
            if aligned:
                w = w.reshape(rows, 3, 2, -1, 2, chunk).transpose(4, 2, 0, 1, 3, 5)
            else:
                w = w.reshape(rows, 3, 2, 2, head_cols).transpose(2, 3, 0, 1, 4)
            return w.reshape(2, 2, rows, 3 * head_cols)

        def qkv_join(w):
            rows = w.shape[2]
            if aligned:
                w = w.reshape(2, 2, rows, 3, -1, chunk).transpose(2, 3, 1, 4, 0, 5)
            else:
                w = w.reshape(2, 2, rows, 3, head_cols).transpose(2, 3, 0, 1, 4)
            return w.reshape(rows, 3 * width)

        ff_rows = down_weight.shape[0]

        def in_split(w):
            rows = w.shape[0]
            w = w.reshape(rows, planes, 2, 2, 2, ff_rows).transpose(2, 4, 0, 1, 3, 5)
            return w.reshape(2, 2, rows, ff_cols)

        def in_join(w):
            rows = w.shape[2]
            w = w.reshape(2, 2, rows, planes, 2, ff_rows).transpose(2, 3, 0, 4, 1, 5)
            return w.reshape(rows, hidden_cols)

        def quad(parts):
            x = exchange(parts, "c")
            return exchange(x.transpose(1, 0, 2, 3), "t")

        def quad_back(x):
            x = exchange(x, "c")
            x = exchange(x.transpose(1, 0, 2, 3), "t")
            return x.transpose(1, 0, 2, 3)

        aux = jnp.concatenate(
            [
                key_mask.astype(f32),
                time_embed.astype(f32),
                jnp.broadcast_to(lengths.astype(f32)[:, None], (1, 128)),
            ],
            axis=1,
        )
        aux_other = over_core(aux)
        aux_both = join(aux[0], aux_other[0], core)
        embed_both = aux_both[:, full_len : full_len + time_embed.shape[1]]
        aux_mine = pick(aux_both, group, 0)
        length = aux_mine[full_len + time_embed.shape[1]].astype(jnp.int32)
        usable = jnp.logical_and(
            aux_mine[:full_len] > 0, jnp.arange(full_len, dtype=jnp.int32) < length
        )

        piece = out_weight.shape[0]

        def out_heads(x):
            x = x.reshape(2, -1, piece, width)
            x = exchange(x, "t")
            return x.transpose(1, 0, 2, 3).reshape(head_cols, width)

        def out_pieces(x):
            x = x.reshape(-1, 2, piece, width).transpose(1, 0, 2, 3)
            return exchange(x, "t").reshape(head_cols, width)

        qkv_scaled = (qkv_weight.astype(f32) * gain_attn.astype(f32)[:, None]).astype(bf16)
        in_scaled = (in_weight.astype(f32) * gain_mlp.astype(f32)[:, None]).astype(bf16)
        w_qkv, labels = gather(quad(qkv_split(qkv_scaled)), ["t", "c"], ["g"])
        gate = w_qkv
        cut = 3 * head_cols // 2
        w_qkv = jnp.concatenate(
            [
                in_order(*gather(w_qkv[..., :cut], labels, forwards)),
                in_order(*gather(w_qkv[..., cut:], labels, backwards)),
            ],
            axis=1,
        )
        if aligned:
            w_out = in_order(*gather(after(out_weight, gate), [], ("g",) + forwards))
            w_out = out_heads(w_out)
        else:
            w_out, labels = gather(out_weight, [], ("c", "t", "g") + forwards)
            w_out = lax.dynamic_slice_in_dim(
                in_order(w_out, labels), (2 * core + side) * head_cols, head_cols, 0
            )
        w_in = in_order(*gather(quad(in_split(after(in_scaled, gate))), ["t", "c"], ("g",) + backwards))
        w_down = in_order(*gather(after(down_weight, gate), [], ("g",) + forwards))

        t_rows = in_order(*gather(time_weight, [], forwards))
        embed_rows = pick(
            pick(embed_both.reshape(2, planes, 2, head_size, -1), core, 2), z, 2
        ).reshape(2, -1)
        part = jnp.dot(
            embed_rows, t_rows.astype(f32), precision=lax.Precision.HIGHEST
        )
        part_mine = pick(part, group, 0) + over_z(pick(part, 1 - group, 0), 2)
        part_mine = part_mine + over_z(part_mine, 1)
        scales = 1.0 + (part_mine + over_core(part_mine))
        scale_attn, scale_mlp = scales[None, :width], scales[None, width:]

        blocks = (
            side + 2 * core,
            side + 2 - 2 * core,
            1 - side + 2 * core,
            1 - side + 2 - 2 * core,
        )
        steps = jnp.arange(span, dtype=jnp.int32)
        valid = (blocks[0] * span + steps < length).astype(f32)[:, None]
        cosine, sine = rope_tables(jnp.concatenate([block * span + steps for block in blocks]), 0)
        usable_blocks = usable.reshape(head_size, span)
        bias = jnp.concatenate([pick(usable_blocks, block, 0) for block in blocks])

        def gather_four(x):
            across = over_z(x, 1)
            return jnp.concatenate([x, over_core(x), across, over_core(across)])

        def sum_four(x):
            x = x.reshape(2, 2, span, width)
            x = x[:, 0] + over_core(x[:, 1].astype(bf16)).astype(f32)
            return x[0] + over_z(x[1].astype(bf16), 1).astype(f32)

        inputs = moved(tokens[0]).astype(f32)
        upstream = moved(after(cotangent[0], gate)).astype(f32)
        white_a, inv_a = whiten(inputs)
        all_a = gather_four((white_a * scale_attn).astype(bf16))
        packed = dot(all_a, w_qkv)
        head_shape = (full_len, head_cols // HD, HD)
        query = rotate(packed[:, :head_cols], cosine, sine).astype(bf16).reshape(head_shape)
        key = rotate(packed[:, head_cols : 2 * head_cols], cosine, sine).astype(bf16)
        key = key.reshape(head_shape)
        value = packed[:, 2 * head_cols :].astype(bf16).reshape(head_shape)
        mixed, log_sum = attend_forward(query, key, value, bias)
        mixed = mixed.reshape(full_len, head_cols)

        hidden = inputs + valid * sum_four(dot(mixed, w_out))
        white_m, inv_m = whiten(hidden)
        all_m = gather_four((white_m * scale_mlp).astype(bf16))
        upper = dot(all_m, w_in)
        phi = 0.5 * (1.0 + lax.erf(upper / math.sqrt(2.0)))
        activation = (upper * phi).astype(bf16)
        slope = phi + upper * jnp.exp(-0.5 * upper * upper) / math.sqrt(2.0 * math.pi)
        output = hidden + valid * sum_four(dot(activation, w_down))
        output = moved(output.astype(bf16))[None]

        all_d = gather_four((valid * upstream).astype(bf16))
        d_upper = (dot_right_t(all_d, w_down) * slope).astype(bf16)
        down_axes = [axis for axis in natural if axis not in ("c", "t")]
        sum_down = reduce_rows(dot_left_t(activation, all_d), down_axes, forwards + ("g",))
        d_normed_m = sum_four(dot_right_t(d_upper, w_in))
        in_sums = reduce_rows(dot_left_t(all_m, d_upper), natural, backwards + ("g",))
        d_from_m, d_scale_m = whiten_back(d_normed_m, white_m, inv_m, scale_mlp)
        d_hidden = upstream + d_from_m
        all_da = gather_four((valid * d_hidden).astype(bf16))
        grad_out = dot_left_t(mixed, all_da).astype(bf16)
        if aligned:
            sum_out = reduce_rows(out_pieces(grad_out), down_axes, forwards + ("g",))
        else:
            padded = lax.dynamic_update_slice_in_dim(
                jnp.zeros((width, width), bf16), grad_out, (2 * core + side) * head_cols, 0
            )
            sum_out = reduce_rows(padded, natural, forwards + ("g", "t", "c"))
        d_mixed = dot_right_t(all_da, w_out).astype(bf16).reshape(head_shape)
        d_query, d_key, d_value = attend_backward(query, key, value, log_sum, d_mixed, bias)
        d_packed = jnp.concatenate(
            [
                rotate(
                    d_query.astype(bf16).astype(f32).reshape(full_len, head_cols), cosine, -sine
                ).astype(bf16),
                rotate(
                    d_key.astype(bf16).astype(f32).reshape(full_len, head_cols), cosine, -sine
                ).astype(bf16),
                d_value.astype(bf16).reshape(full_len, head_cols),
            ],
            axis=1,
        )
        grad_qkv = dot_left_t(all_a, d_packed)
        qkv_sums = jnp.concatenate(
            [
                reduce_rows(grad_qkv[:, :cut], natural, forwards + ("g",)),
                reduce_rows(grad_qkv[:, cut:], natural, backwards + ("g",)),
            ],
            axis=-1,
        )
        d_normed_a = sum_four(dot_right_t(d_packed, w_qkv))
        d_from_a, d_scale_a = whiten_back(d_normed_a, white_a, inv_a, scale_attn)
        grad_tokens = moved((d_hidden + d_from_a).astype(bf16))[None]

        raw_qkv = qkv_join(quad_back(qkv_sums.astype(bf16))).astype(f32)
        raw_in = in_join(quad_back(in_sums.astype(bf16))).astype(f32)
        sum_gain_a = jnp.sum(raw_qkv * qkv_weight.astype(f32), axis=1)
        sum_gain_m = jnp.sum(raw_in * in_weight.astype(f32), axis=1)
        sum_qkv = raw_qkv * gain_attn.astype(f32)[:, None]
        sum_in = raw_in * gain_mlp.astype(f32)[:, None]

        d_scale = jnp.concatenate([d_scale_a, d_scale_m], axis=1)
        d_scale = d_scale + over_core(d_scale)
        d_scale = d_scale + over_z(d_scale, 1)
        d_both = join(d_scale[0], over_z(d_scale, 2)[0], group)
        rows_time = lax.dot_general(
            embed_rows,
            d_both,
            (((0,), (0,)), ((), ())),
            precision=lax.Precision.HIGHEST,
            preferred_element_type=f32,
        ).reshape((2,) * plane_bits + (-1, 2 * width))
        alive = list(backwards)
        for axis in backwards:
            at, mine = alive.index(axis), where[axis]
            rows_time = pick(rows_time, mine, at) + send(pick(rows_time, 1 - mine, at), axis)
            alive.remove(axis)
        return (
            output,
            grad_tokens,
            rows_time,
            sum_gain_a,
            sum_qkv,
            sum_out,
            sum_gain_m,
            sum_in,
            sum_down,
        )

    return per_device


def solution(mesh):
    rows, both, flat = P(("seq", "head"), None), P("seq", "head", None), P(("seq", "head"))
    return jax.shard_map(
        build(mesh.shape["seq"], mesh.shape["head"]),
        mesh=mesh,
        in_specs=(both, both, P("seq", None), P("seq"), P("seq", None), rows, flat, rows, rows, flat, rows, rows),
        out_specs=(both, both, rows, flat, rows, rows, flat, rows, rows),
        check_vma=False,
    )
```

```python
import math

import jax
import jax.numpy as jnp
from jax import lax
from jax.sharding import Mesh
from jax.sharding import PartitionSpec as P

HEADS = 16
HD = 64

epsilon = 1e-05
f32 = jnp.float32
bf16 = jnp.bfloat16


def dot(left, right):
    return jnp.dot(left, right, preferred_element_type=f32)


def dot_right_t(left, right):
    return lax.dot_general(left, right, (((1,), (1,)), ((), ())), preferred_element_type=f32)


def dot_left_t(left, right):
    return lax.dot_general(left, right, (((0,), (0,)), ((), ())), preferred_element_type=f32)


def whiten(field):
    centre = jnp.mean(field, axis=-1, keepdims=True)
    shifted = field - centre
    variance = jnp.mean(shifted * shifted, axis=-1, keepdims=True)
    inv_std = lax.rsqrt(variance + epsilon)
    return shifted * inv_std, inv_std


def whiten_back(d_normed, whitened, inv_std, scale_vec):
    d_scale = jnp.sum(d_normed * whitened, axis=0, keepdims=True)
    d_white = d_normed * scale_vec
    d_input = inv_std * (
        d_white
        - jnp.mean(d_white, axis=-1, keepdims=True)
        - whitened * jnp.mean(d_white * whitened, axis=-1, keepdims=True)
    )
    return d_input, d_scale


def rope_tables(positions, repeats):
    half_dim = HD // 2
    inverse_freq = jnp.power(10000.0, -jnp.arange(half_dim, dtype=f32) * 2.0 / HD)
    angles = positions.astype(f32)[:, None] * inverse_freq[None, :]
    return jnp.cos(angles)[:, None, :], jnp.sin(angles)[:, None, :]


def rotate(field, cosine, sine):
    rows, width = field.shape
    field = field.reshape(rows, width // HD, HD)
    half_dim = HD // 2
    first, second = field[..., :half_dim], field[..., half_dim:]
    turned = jnp.concatenate(
        [first * cosine - second * sine, second * cosine + first * sine], axis=-1
    )
    return turned.reshape(rows, width)


def attend_forward(query, key, value, bias):
    length = query.shape[0]
    block = min(512, length)
    scale = 1.0 / math.sqrt(HD)
    mixed, logs = [], []
    for at in range(0, length, block):
        scores = jnp.einsum("qhd,khd->hqk", query[at : at + block], key, preferred_element_type=f32)
        scores = jnp.where(bias[None, None, :], scores * scale, -1e30)
        row_max = jnp.max(scores, axis=-1, keepdims=True)
        weights = jnp.exp(scores - row_max)
        row_sum = jnp.sum(weights, axis=-1, keepdims=True)
        low = (weights / row_sum).astype(bf16)
        mixed.append(
            jnp.einsum("hqk,khd->qhd", low, value, preferred_element_type=f32).astype(bf16)
        )
        logs.append((row_max + jnp.log(row_sum))[..., 0])
    return jnp.concatenate(mixed, axis=0), jnp.concatenate(logs, axis=1)


def attend_backward(query, key, value, log_sum, d_out, bias):
    length = query.shape[0]
    block = min(512, length)
    scale = 1.0 / math.sqrt(HD)
    d_key = jnp.zeros(key.shape, f32)
    d_value = jnp.zeros(value.shape, f32)
    d_query = []
    for at in range(0, length, block):
        q_block, d_block = query[at : at + block], d_out[at : at + block]
        scores = jnp.einsum("qhd,khd->hqk", q_block, key, preferred_element_type=f32) * scale
        scores = jnp.where(bias[None, None, :], scores, -1e30)
        probs = jnp.exp(scores - log_sum[:, at : at + block, None])
        low = probs.astype(bf16)
        d_value = d_value + jnp.einsum("hqk,qhd->khd", low, d_block, preferred_element_type=f32)
        d_probs = jnp.einsum("qhd,khd->hqk", d_block, value, preferred_element_type=f32)
        row_dot = jnp.sum(d_probs * probs, axis=-1, keepdims=True)
        d_scores = (probs * (d_probs - row_dot)).astype(bf16)
        d_query.append(
            jnp.einsum("hqk,khd->qhd", d_scores, key, preferred_element_type=f32) * scale
        )
        d_key = d_key + scale * jnp.einsum(
            "hqk,qhd->khd", d_scores, q_block, preferred_element_type=f32
        )
    return jnp.concatenate(d_query, axis=0), d_key, d_value


def build(seq_size, head_size):
    plane_bits = (seq_size // 2).bit_length() - 1
    planes = seq_size // 2
    assert planes == 1 << plane_bits and seq_size >= 2 and head_size == 4

    def swap(x, axis, mask, size):
        return lax.ppermute(x, axis, [(i, i ^ mask) for i in range(size)])

    def pick(x, index, axis):
        return lax.dynamic_index_in_dim(x, index, axis, keepdims=False)

    def join(own, other, bit, axis=0):
        return jnp.where(
            bit == 0, jnp.stack([own, other], axis=axis), jnp.stack([other, own], axis=axis)
        )

    def per_device(
        tokens,
        cotangent,
        time_embed,
        lengths,
        key_mask,
        time_weight,
        gain_attn,
        qkv_weight,
        out_weight,
        gain_mlp,
        in_weight,
        down_weight,
    ):
        core, plane = lax.axis_index("core"), lax.axis_index("plane")
        group, side = lax.axis_index("group"), lax.axis_index("side")
        stays = core == group
        _, span, width = tokens.shape
        full_len = span * head_size
        hidden_cols = in_weight.shape[1]
        head_cols, ff_cols = width // 4, hidden_cols // 4
        forwards = tuple(range(plane_bits))
        backwards = tuple(reversed(forwards))
        where = {"c": core, "g": group, "t": side}
        where.update({bit: (plane >> bit) & 1 for bit in range(plane_bits)})
        natural = list(backwards) + ["c", "g", "t"]

        def send(x, axis):
            if axis in ("c", "g", "t"):
                name = {"c": "core", "g": "group", "t": "side"}[axis]
                return swap(x, name, 1, 2)
            return swap(x, "plane", 1 << axis, planes)

        def moved(x):
            return jnp.where(stays, x, lax.ppermute(x, ("core", "group"), [(1, 2), (2, 1)]))

        def after(x, first):
            return lax.optimization_barrier((x, first))[0]

        def gather(x, labels, axes):
            for axis in axes:
                x = join(x, send(x, axis), where[axis])
                labels = [axis] + labels
            return x, labels

        def in_order(x, labels):
            wanted = [axis for axis in natural if axis in labels]
            perm = [labels.index(axis) for axis in wanted]
            x = x.transpose(perm + list(range(len(perm), x.ndim)))
            return x.reshape(-1, x.shape[-1])

        def exchange(parts, axis):
            mine = where[axis]
            return join(pick(parts, mine, 0), send(pick(parts, 1 - mine, 0), axis), mine)

        def reduce_rows(x, labels, axes):
            labels = [axis for axis in natural if axis in labels]
            y = x.astype(bf16).reshape((2,) * len(labels) + (-1, x.shape[-1]))
            for step, axis in enumerate(axes):
                at, mine = labels.index(axis), where[axis]
                other = send(pick(y, 1 - mine, at), axis)
                y = pick(y, mine, at).astype(f32) + other.astype(f32)
                if step + 1 < len(axes):
                    y = y.astype(bf16)
                labels.remove(axis)
            return y

        chunk = out_weight.shape[0] * head_size
        aligned = (chunk % HD == 0) and (width // (2 * chunk)) % 2 == 0

        def qkv_split(w):
            rows = w.shape[0]
            if aligned:
                w = w.reshape(rows, 3, 2, -1, 2, chunk).transpose(4, 2, 0, 1, 3, 5)
            else:
                w = w.reshape(rows, 3, 2, 2, head_cols).transpose(2, 3, 0, 1, 4)
            return w.reshape(2, 2, rows, 3 * head_cols)

        def qkv_join(w):
            rows = w.shape[2]
            if aligned:
                w = w.reshape(2, 2, rows, 3, -1, chunk).transpose(2, 3, 1, 4, 0, 5)
            else:
                w = w.reshape(2, 2, rows, 3, head_cols).transpose(2, 3, 0, 1, 4)
            return w.reshape(rows, 3 * width)

        ff_rows = down_weight.shape[0]

        def in_split(w):
            rows = w.shape[0]
            w = w.reshape(rows, planes, 2, 2, 2, ff_rows).transpose(2, 4, 0, 1, 3, 5)
            return w.reshape(2, 2, rows, ff_cols)

        def in_join(w):
            rows = w.shape[2]
            w = w.reshape(2, 2, rows, planes, 2, ff_rows).transpose(2, 3, 0, 4, 1, 5)
            return w.reshape(rows, hidden_cols)

        def quad(parts):
            x = exchange(parts, "c")
            return exchange(x.transpose(1, 0, 2, 3), "t")

        def quad_back(x):
            x = exchange(x, "c")
            x = exchange(x.transpose(1, 0, 2, 3), "t")
            return x.transpose(1, 0, 2, 3)

        aux = jnp.concatenate(
            [
                key_mask.astype(f32),
                time_embed.astype(f32),
                jnp.broadcast_to(lengths.astype(f32)[:, None], (1, 128)),
            ],
            axis=1,
        )
        aux_other = send(aux, "c")
        aux_both = join(aux[0], aux_other[0], core)
        embed_both = aux_both[:, full_len : full_len + time_embed.shape[1]]
        aux_mine = pick(aux_both, group, 0)
        length = aux_mine[full_len + time_embed.shape[1]].astype(jnp.int32)
        usable = jnp.logical_and(
            aux_mine[:full_len] > 0, jnp.arange(full_len, dtype=jnp.int32) < length
        )

        piece = out_weight.shape[0]

        def out_heads(x):
            x = x.reshape(2, -1, piece, width)
            x = exchange(x, "t")
            return x.transpose(1, 0, 2, 3).reshape(head_cols, width)

        def out_pieces(x):
            x = x.reshape(-1, 2, piece, width).transpose(1, 0, 2, 3)
            return exchange(x, "t").reshape(head_cols, width)

        qkv_scaled = (qkv_weight.astype(f32) * gain_attn.astype(f32)[:, None]).astype(bf16)
        in_scaled = (in_weight.astype(f32) * gain_mlp.astype(f32)[:, None]).astype(bf16)
        qkv_quad = quad(qkv_split(qkv_scaled))
        w_qkv, labels = gather(qkv_quad, ["t", "c"], ["g"])
        gate = w_qkv
        cut = 3 * head_cols // 2
        w_qkv = jnp.concatenate(
            [
                in_order(*gather(w_qkv[..., :cut], labels, forwards)),
                in_order(*gather(w_qkv[..., cut:], labels, backwards)),
            ],
            axis=1,
        )
        in_quad = quad(in_split(after(in_scaled, qkv_quad)))
        rows_in = 4 * in_weight.shape[0]
        packs = [in_quad.reshape(rows_in, width), down_weight] + ([out_weight] if aligned else [])
        packs = lax.all_gather(jnp.concatenate(packs), ("plane", "group"), axis=0)
        w_in = packs[:, :rows_in].reshape(planes, 2, 2, 2, -1, width)
        w_in = w_in.transpose(0, 3, 1, 2, 4, 5).reshape(width, ff_cols)
        w_down = packs[:, rows_in : rows_in + ff_rows].reshape(ff_cols, width)
        if aligned:
            w_out = out_heads(packs[:, rows_in + ff_rows :])
        else:
            w_out, labels = gather(out_weight, [], ("c", "t", "g") + forwards)
            w_out = lax.dynamic_slice_in_dim(
                in_order(w_out, labels), (2 * core + side) * head_cols, head_cols, 0
            )

        t_rows, labels = gather(after(time_weight, qkv_quad), [], forwards[:1])
        t_rows = in_order(*gather(after(t_rows, gate), labels, forwards[1:]))
        embed_rows = pick(
            pick(embed_both.reshape(2, planes, 2, head_size, -1), core, 2), 2 * group + side, 2
        ).reshape(2, -1)
        part = jnp.dot(
            embed_rows, t_rows.astype(f32), precision=lax.Precision.HIGHEST
        )
        part_mine = pick(part, group, 0) + send(pick(part, 1 - group, 0), "g")
        part_mine = part_mine + send(part_mine, "t")
        scales = 1.0 + (part_mine + send(part_mine, "c"))
        scale_attn, scale_mlp = scales[None, :width], scales[None, width:]

        blocks = (
            side + 2 * core,
            side + 2 - 2 * core,
            1 - side + 2 * core,
            1 - side + 2 - 2 * core,
        )
        steps = jnp.arange(span, dtype=jnp.int32)
        valid = (blocks[0] * span + steps < length).astype(f32)[:, None]
        cosine, sine = rope_tables(jnp.concatenate([block * span + steps for block in blocks]), 0)
        usable_blocks = usable.reshape(head_size, span)
        bias = jnp.concatenate([pick(usable_blocks, block, 0) for block in blocks])

        def gather_four(x):
            across = send(x, "t")
            return jnp.concatenate([x, send(x, "c"), across, send(across, "c")])

        def sum_four(x):
            x = x.reshape(2, 2, span, width)
            x = x[:, 0] + send(x[:, 1].astype(bf16), "c").astype(f32)
            return x[0] + send(x[1].astype(bf16), "t").astype(f32)

        inputs = moved(tokens[0]).astype(f32)
        upstream = moved(after(cotangent[0], gate)).astype(f32)
        white_a, inv_a = whiten(inputs)
        all_a = gather_four((white_a * scale_attn).astype(bf16))
        packed = dot(all_a, w_qkv)
        head_shape = (full_len, head_cols // HD, HD)
        query = rotate(packed[:, :head_cols], cosine, sine).astype(bf16).reshape(head_shape)
        key = rotate(packed[:, head_cols : 2 * head_cols], cosine, sine).astype(bf16)
        key = key.reshape(head_shape)
        value = packed[:, 2 * head_cols :].astype(bf16).reshape(head_shape)
        mixed, log_sum = attend_forward(query, key, value, bias)
        mixed = mixed.reshape(full_len, head_cols)

        hidden = inputs + valid * sum_four(dot(mixed, w_out))
        white_m, inv_m = whiten(hidden)
        all_m = gather_four((white_m * scale_mlp).astype(bf16))
        upper = dot(all_m, w_in)
        phi = 0.5 * (1.0 + lax.erf(upper / math.sqrt(2.0)))
        activation = (upper * phi).astype(bf16)
        slope = phi + upper * jnp.exp(-0.5 * upper * upper) / math.sqrt(2.0 * math.pi)
        activation, slope = lax.optimization_barrier((activation, slope))
        output = hidden + valid * sum_four(dot(activation, w_down))
        output = moved(output.astype(bf16))[None]

        all_d = gather_four((valid * upstream).astype(bf16))
        d_upper = (dot_right_t(all_d, w_down) * slope).astype(bf16)
        down_axes = [axis for axis in natural if axis not in ("c", "t")]
        grad_down = dot_left_t(activation, all_d).astype(bf16).reshape(planes, 2 * ff_rows, width)
        d_normed_m = sum_four(dot_right_t(d_upper, w_in))
        grad_in = dot_left_t(all_m, d_upper).astype(bf16).reshape(planes, 2 * rows_in, width)
        both = lax.psum_scatter(
            jnp.concatenate([grad_in, grad_down], axis=1), "plane", scatter_dimension=0, tiled=True
        )[0]
        both_in = both[: 2 * rows_in].reshape(2, 2, 2, -1, width).transpose(1, 0, 2, 3, 4)
        both = jnp.concatenate(
            [both_in.reshape(2, rows_in, width), both[2 * rows_in :].reshape(2, ff_rows, width)],
            axis=1,
        )
        both = pick(both, group, 0).astype(f32) + send(pick(both, 1 - group, 0), "g").astype(f32)
        in_sums = both[:rows_in].reshape(2, 2, -1, width)
        sum_down = both[rows_in:]
        d_from_m, d_scale_m = whiten_back(d_normed_m, white_m, inv_m, scale_mlp)
        d_hidden = upstream + d_from_m
        all_da = gather_four((valid * d_hidden).astype(bf16))
        grad_out = dot_left_t(mixed, all_da).astype(bf16)
        if aligned:
            out_rows = out_pieces(grad_out).reshape(planes, -1, width)
            out_rows = lax.psum_scatter(out_rows, "plane", scatter_dimension=0, tiled=True)
            sum_out = reduce_rows(out_rows[0], ["g"], ["g"])
        else:
            padded = lax.dynamic_update_slice_in_dim(
                jnp.zeros((width, width), bf16), grad_out, (2 * core + side) * head_cols, 0
            )
            sum_out = reduce_rows(padded, natural, forwards + ("g", "t", "c"))
        d_mixed = dot_right_t(all_da, w_out).astype(bf16).reshape(head_shape)
        d_query, d_key, d_value = attend_backward(query, key, value, log_sum, d_mixed, bias)
        d_packed = jnp.concatenate(
            [
                rotate(
                    d_query.astype(bf16).astype(f32).reshape(full_len, head_cols), cosine, -sine
                ).astype(bf16),
                rotate(
                    d_key.astype(bf16).astype(f32).reshape(full_len, head_cols), cosine, -sine
                ).astype(bf16),
                d_value.astype(bf16).reshape(full_len, head_cols),
            ],
            axis=1,
        )
        grad_qkv = dot_left_t(all_a, d_packed)
        qkv_sums = jnp.concatenate(
            [
                reduce_rows(grad_qkv[:, :cut], natural, forwards + ("g",)),
                reduce_rows(grad_qkv[:, cut:], natural, backwards + ("g",)),
            ],
            axis=-1,
        )
        d_normed_a = sum_four(dot_right_t(d_packed, w_qkv))
        d_from_a, d_scale_a = whiten_back(d_normed_a, white_a, inv_a, scale_attn)
        grad_tokens = moved((d_hidden + d_from_a).astype(bf16))[None]

        raw_qkv = qkv_join(quad_back(qkv_sums.astype(bf16))).astype(f32)
        raw_in = in_join(quad_back(in_sums.astype(bf16))).astype(f32)
        sum_gain_a = jnp.sum(raw_qkv * qkv_weight.astype(f32), axis=1)
        sum_gain_m = jnp.sum(raw_in * in_weight.astype(f32), axis=1)
        sum_qkv = raw_qkv * gain_attn.astype(f32)[:, None]
        sum_in = raw_in * gain_mlp.astype(f32)[:, None]

        d_scale = jnp.concatenate([d_scale_a, d_scale_m], axis=1)
        d_scale = d_scale + send(d_scale, "c")
        d_scale = d_scale + send(d_scale, "t")
        d_both = join(d_scale[0], send(d_scale, "g")[0], group)
        rows_time = lax.dot_general(
            embed_rows,
            d_both,
            (((0,), (0,)), ((), ())),
            precision=lax.Precision.HIGHEST,
            preferred_element_type=f32,
        ).reshape((2,) * plane_bits + (-1, 2 * width))
        alive = list(backwards)
        for axis in backwards:
            at, mine = alive.index(axis), where[axis]
            rows_time = pick(rows_time, mine, at) + send(pick(rows_time, 1 - mine, at), axis)
            alive.remove(axis)
        return (
            output,
            grad_tokens,
            rows_time,
            sum_gain_a,
            sum_qkv,
            sum_out,
            sum_gain_m,
            sum_in,
            sum_down,
        )

    return per_device


def solution(mesh):
    seq_size, head_size = mesh.shape["seq"], mesh.shape["head"]
    own_mesh = Mesh(
        mesh.devices.reshape(seq_size // 2, 2, 2, head_size // 2),
        ("plane", "core", "group", "side"),
    )
    seq, head = ("plane", "core"), ("group", "side")
    rows, both, flat = P(seq + head, None), P(seq, head, None), P(seq + head)
    return jax.shard_map(
        build(seq_size, head_size),
        mesh=own_mesh,
        in_specs=(
            both,
            both,
            P(seq, None),
            P(seq),
            P(seq, None),
            rows,
            flat,
            rows,
            rows,
            flat,
            rows,
            rows,
        ),
        out_specs=(both, both, rows, flat, rows, rows, flat, rows, rows),
        check_vma=False,
    )
```

```python
import math

import jax
import jax.numpy as jnp
from jax import lax
from jax.sharding import Mesh
from jax.sharding import PartitionSpec as P

HEADS = 16
HD = 64

epsilon = 1e-05
f32 = jnp.float32
bf16 = jnp.bfloat16


def dot(left, right):
    return jnp.dot(left, right, preferred_element_type=f32)


def dot_right_t(left, right):
    return lax.dot_general(left, right, (((1,), (1,)), ((), ())), preferred_element_type=f32)


def dot_left_t(left, right):
    return lax.dot_general(left, right, (((0,), (0,)), ((), ())), preferred_element_type=f32)


def whiten(field):
    centre = jnp.mean(field, axis=-1, keepdims=True)
    shifted = field - centre
    variance = jnp.mean(shifted * shifted, axis=-1, keepdims=True)
    inv_std = lax.rsqrt(variance + epsilon)
    return shifted * inv_std, inv_std


def whiten_back(d_normed, whitened, inv_std, scale_vec):
    d_scale = jnp.sum(d_normed * whitened, axis=0, keepdims=True)
    d_white = d_normed * scale_vec
    d_input = inv_std * (
        d_white
        - jnp.mean(d_white, axis=-1, keepdims=True)
        - whitened * jnp.mean(d_white * whitened, axis=-1, keepdims=True)
    )
    return d_input, d_scale


def rope_tables(positions, repeats):
    half_dim = HD // 2
    inverse_freq = jnp.power(10000.0, -jnp.arange(half_dim, dtype=f32) * 2.0 / HD)
    angles = positions.astype(f32)[:, None] * inverse_freq[None, :]
    return jnp.cos(angles)[:, None, :], jnp.sin(angles)[:, None, :]


def rotate(field, cosine, sine):
    rows, width = field.shape
    field = field.reshape(rows, width // HD, HD)
    half_dim = HD // 2
    first, second = field[..., :half_dim], field[..., half_dim:]
    turned = jnp.concatenate(
        [first * cosine - second * sine, second * cosine + first * sine], axis=-1
    )
    return turned.reshape(rows, width)


def attend_forward(query, key, value, bias):
    length = query.shape[0]
    block = min(512, length)
    scale = 1.0 / math.sqrt(HD)
    mixed, logs = [], []
    for at in range(0, length, block):
        scores = jnp.einsum("qhd,khd->hqk", query[at : at + block], key, preferred_element_type=f32)
        scores = jnp.where(bias[None, None, :], scores * scale, -1e30)
        row_max = jnp.max(scores, axis=-1, keepdims=True)
        weights = jnp.exp(scores - row_max)
        row_sum = jnp.sum(weights, axis=-1, keepdims=True)
        low = (weights / row_sum).astype(bf16)
        mixed.append(
            jnp.einsum("hqk,khd->qhd", low, value, preferred_element_type=f32).astype(bf16)
        )
        logs.append((row_max + jnp.log(row_sum))[..., 0])
    return jnp.concatenate(mixed, axis=0), jnp.concatenate(logs, axis=1)


def attend_backward(query, key, value, log_sum, d_out, bias):
    length = query.shape[0]
    block = min(512, length)
    scale = 1.0 / math.sqrt(HD)
    d_key = jnp.zeros(key.shape, f32)
    d_value = jnp.zeros(value.shape, f32)
    d_query = []
    for at in range(0, length, block):
        q_block, d_block = query[at : at + block], d_out[at : at + block]
        scores = jnp.einsum("qhd,khd->hqk", q_block, key, preferred_element_type=f32) * scale
        scores = jnp.where(bias[None, None, :], scores, -1e30)
        probs = jnp.exp(scores - log_sum[:, at : at + block, None])
        low = probs.astype(bf16)
        d_value = d_value + jnp.einsum("hqk,qhd->khd", low, d_block, preferred_element_type=f32)
        d_probs = jnp.einsum("qhd,khd->hqk", d_block, value, preferred_element_type=f32)
        row_dot = jnp.sum(d_probs * probs, axis=-1, keepdims=True)
        d_scores = (probs * (d_probs - row_dot)).astype(bf16)
        d_query.append(
            jnp.einsum("hqk,khd->qhd", d_scores, key, preferred_element_type=f32) * scale
        )
        d_key = d_key + scale * jnp.einsum(
            "hqk,qhd->khd", d_scores, q_block, preferred_element_type=f32
        )
    return jnp.concatenate(d_query, axis=0), d_key, d_value


def build(seq_size, head_size):
    plane_bits = (seq_size // 2).bit_length() - 1
    planes = seq_size // 2
    assert planes == 1 << plane_bits and seq_size >= 2 and head_size == 4

    def swap(x, axis, mask, size):
        return lax.ppermute(x, axis, [(i, i ^ mask) for i in range(size)])

    def pick(x, index, axis):
        return lax.dynamic_index_in_dim(x, index, axis, keepdims=False)

    def join(own, other, bit, axis=0):
        return jnp.where(
            bit == 0, jnp.stack([own, other], axis=axis), jnp.stack([other, own], axis=axis)
        )

    def per_device(
        tokens,
        cotangent,
        time_embed,
        lengths,
        key_mask,
        time_weight,
        gain_attn,
        qkv_weight,
        out_weight,
        gain_mlp,
        in_weight,
        down_weight,
    ):
        core, plane = lax.axis_index("core"), lax.axis_index("plane")
        group, side = lax.axis_index("group"), lax.axis_index("side")
        stays = core == group
        _, span, width = tokens.shape
        full_len = span * head_size
        hidden_cols = in_weight.shape[1]
        head_cols, ff_cols = width // 4, hidden_cols // 4
        forwards = tuple(range(plane_bits))
        backwards = tuple(reversed(forwards))
        where = {"c": core, "g": group, "t": side}
        where.update({bit: (plane >> bit) & 1 for bit in range(plane_bits)})
        natural = list(backwards) + ["c", "g", "t"]

        def send(x, axis):
            if axis in ("c", "g", "t"):
                name = {"c": "core", "g": "group", "t": "side"}[axis]
                return swap(x, name, 1, 2)
            return swap(x, "plane", 1 << axis, planes)

        def moved(x):
            return jnp.where(stays, x, lax.ppermute(x, ("core", "group"), [(1, 2), (2, 1)]))

        def after(x, first):
            return lax.optimization_barrier((x, first))

        def gather(x, labels, axes):
            for axis in axes:
                x = join(x, send(x, axis), where[axis])
                labels = [axis] + labels
            return x, labels

        def in_order(x, labels):
            wanted = [axis for axis in natural if axis in labels]
            perm = [labels.index(axis) for axis in wanted]
            x = x.transpose(perm + list(range(len(perm), x.ndim)))
            return x.reshape(-1, x.shape[-1])

        def exchange(parts, axis):
            mine = where[axis]
            return join(pick(parts, mine, 0), send(pick(parts, 1 - mine, 0), axis), mine)

        def reduce_rows(x, labels, axes):
            labels = [axis for axis in natural if axis in labels]
            y = x.astype(bf16).reshape((2,) * len(labels) + (-1, x.shape[-1]))
            for step, axis in enumerate(axes):
                at, mine = labels.index(axis), where[axis]
                other = send(pick(y, 1 - mine, at), axis)
                y = pick(y, mine, at).astype(f32) + other.astype(f32)
                if step + 1 < len(axes):
                    y = y.astype(bf16)
                labels.remove(axis)
            return y

        chunk = out_weight.shape[0] * head_size
        aligned = (chunk % HD == 0) and (width // (2 * chunk)) % 2 == 0

        def qkv_split(w):
            rows = w.shape[0]
            if aligned:
                w = w.reshape(rows, 3, 2, -1, 2, chunk).transpose(4, 2, 0, 1, 3, 5)
            else:
                w = w.reshape(rows, 3, 2, 2, head_cols).transpose(2, 3, 0, 1, 4)
            return w.reshape(2, 2, rows, 3 * head_cols)

        def qkv_join(w):
            rows = w.shape[2]
            if aligned:
                w = w.reshape(2, 2, rows, 3, -1, chunk).transpose(2, 3, 1, 4, 0, 5)
            else:
                w = w.reshape(2, 2, rows, 3, head_cols).transpose(2, 3, 0, 1, 4)
            return w.reshape(rows, 3 * width)

        ff_rows = down_weight.shape[0]

        def in_split(w):
            rows = w.shape[0]
            w = w.reshape(rows, planes, 2, 2, 2, ff_rows).transpose(2, 4, 0, 1, 3, 5)
            return w.reshape(2, 2, rows, ff_cols)

        def in_join(w):
            rows = w.shape[2]
            w = w.reshape(2, 2, rows, planes, 2, ff_rows).transpose(2, 3, 0, 4, 1, 5)
            return w.reshape(rows, hidden_cols)

        def quad(parts):
            x = exchange(parts, "c")
            return exchange(x.transpose(1, 0, 2, 3), "t"), x

        def quad_back(x):
            x = exchange(x, "c")
            x = exchange(x.transpose(1, 0, 2, 3), "t")
            return x.transpose(1, 0, 2, 3)

        aux = jnp.concatenate(
            [
                key_mask.astype(f32),
                time_embed.astype(f32),
                jnp.broadcast_to(lengths.astype(f32)[:, None], (1, 128)),
            ],
            axis=1,
        )
        aux_other = send(aux, "c")
        aux_both = join(aux[0], aux_other[0], core)
        embed_both = aux_both[:, full_len : full_len + time_embed.shape[1]]
        aux_mine = pick(aux_both, group, 0)
        length = aux_mine[full_len + time_embed.shape[1]].astype(jnp.int32)
        usable = jnp.logical_and(
            aux_mine[:full_len] > 0, jnp.arange(full_len, dtype=jnp.int32) < length
        )

        piece = out_weight.shape[0]

        def out_heads(x):
            x = x.reshape(2, -1, piece, width)
            x = exchange(x, "t")
            return x.transpose(1, 0, 2, 3).reshape(head_cols, width)

        def out_pieces(x):
            x = x.reshape(-1, 2, piece, width).transpose(1, 0, 2, 3)
            return exchange(x, "t").reshape(head_cols, width)

        qkv_scaled = (qkv_weight.astype(f32) * gain_attn.astype(f32)[:, None]).astype(bf16)
        in_scaled = (in_weight.astype(f32) * gain_mlp.astype(f32)[:, None]).astype(bf16)
        qkv_quad, _ = quad(qkv_split(qkv_scaled))
        time_rows, qkv_quad = after(time_weight, qkv_quad)
        w_qkv, labels = gather(qkv_quad, ["t", "c"], ["g"])
        later, w_qkv = after(cotangent[0], w_qkv)
        cut = 3 * head_cols // 2
        w_qkv = jnp.concatenate(
            [
                in_order(*gather(w_qkv[..., :cut], labels, forwards)),
                in_order(*gather(w_qkv[..., cut:], labels, backwards)),
            ],
            axis=1,
        )
        in_quad, _ = quad(in_split(in_scaled))
        rows_in = 4 * in_weight.shape[0]
        packs = [in_quad.reshape(rows_in, width), down_weight] + ([out_weight] if aligned else [])
        packs = lax.all_gather(jnp.concatenate(packs), ("plane", "group"), axis=0)
        w_in = packs[:, :rows_in].reshape(planes, 2, 2, 2, -1, width)
        w_in = w_in.transpose(0, 3, 1, 2, 4, 5).reshape(width, ff_cols)
        w_down = packs[:, rows_in : rows_in + ff_rows].reshape(ff_cols, width)
        if aligned:
            w_out = out_heads(packs[:, rows_in + ff_rows :])
        else:
            w_out, labels = gather(out_weight, [], ("c", "t", "g") + forwards)
            w_out = lax.dynamic_slice_in_dim(
                in_order(w_out, labels), (2 * core + side) * head_cols, head_cols, 0
            )

        t_rows, labels = gather(time_rows, [], forwards[:1])
        t_rows = in_order(*gather(t_rows, labels, forwards[1:]))
        embed_rows = pick(
            pick(embed_both.reshape(2, planes, 2, head_size, -1), core, 2), 2 * group + side, 2
        ).reshape(2, -1)
        part = jnp.dot(
            embed_rows, t_rows.astype(f32), precision=lax.Precision.HIGHEST
        )
        part_mine = pick(part, group, 0) + send(pick(part, 1 - group, 0), "g")
        part_mine = part_mine + send(part_mine, "t")
        scales = 1.0 + (part_mine + send(part_mine, "c"))
        scale_attn, scale_mlp = scales[None, :width], scales[None, width:]

        blocks = (
            side + 2 * core,
            side + 2 - 2 * core,
            1 - side + 2 * core,
            1 - side + 2 - 2 * core,
        )
        steps = jnp.arange(span, dtype=jnp.int32)
        valid = (blocks[0] * span + steps < length).astype(f32)[:, None]
        cosine, sine = rope_tables(jnp.concatenate([block * span + steps for block in blocks]), 0)
        usable_blocks = usable.reshape(head_size, span)
        bias = jnp.concatenate([pick(usable_blocks, block, 0) for block in blocks])

        def gather_four(x):
            across = send(x, "t")
            return jnp.concatenate([x, send(x, "c"), across, send(across, "c")])

        def sum_four(x):
            x = x.reshape(2, 2, span, width)
            x = x[:, 0] + send(x[:, 1].astype(bf16), "c").astype(f32)
            return x[0] + send(x[1].astype(bf16), "t").astype(f32)

        inputs = moved(tokens[0]).astype(f32)
        w_qkv, upstream = after(w_qkv, moved(later))
        upstream = upstream.astype(f32)
        all_d = gather_four((valid * upstream).astype(bf16))
        w_out, all_d = after(w_out, all_d)
        white_a, inv_a = whiten(inputs)
        all_a = gather_four((white_a * scale_attn).astype(bf16))
        packed = dot(all_a, w_qkv)
        head_shape = (full_len, head_cols // HD, HD)
        query = rotate(packed[:, :head_cols], cosine, sine).astype(bf16).reshape(head_shape)
        key = rotate(packed[:, head_cols : 2 * head_cols], cosine, sine).astype(bf16)
        key = key.reshape(head_shape)
        value = packed[:, 2 * head_cols :].astype(bf16).reshape(head_shape)
        mixed, log_sum = attend_forward(query, key, value, bias)
        mixed = mixed.reshape(full_len, head_cols)

        hidden = inputs + valid * sum_four(dot(mixed, w_out))
        white_m, inv_m = whiten(hidden)
        all_m = gather_four((white_m * scale_mlp).astype(bf16))
        upper = dot(all_m, w_in)
        phi = 0.5 * (1.0 + lax.erf(upper / math.sqrt(2.0)))
        activation = (upper * phi).astype(bf16)
        slope = phi + upper * jnp.exp(-0.5 * upper * upper) / math.sqrt(2.0 * math.pi)
        activation, slope = lax.optimization_barrier((activation, slope))
        mlp_part = dot(activation, w_down).astype(bf16)

        d_upper = (dot_right_t(all_d, w_down) * slope).astype(bf16)
        down_axes = [axis for axis in natural if axis not in ("c", "t")]
        grad_down = dot_left_t(activation, all_d).astype(bf16).reshape(planes, 2 * ff_rows, width)
        d_normed_m = sum_four(dot_right_t(d_upper, w_in))
        grad_in = dot_left_t(all_m, d_upper).astype(bf16).reshape(planes, 2 * rows_in, width)
        sum_d = lax.psum_scatter(grad_down, "plane", scatter_dimension=0, tiled=True)[0]
        sum_i = lax.psum_scatter(grad_in, "plane", scatter_dimension=0, tiled=True)[0]
        both = jnp.concatenate([sum_i, sum_d])
        both_in = both[: 2 * rows_in].reshape(2, 2, 2, -1, width).transpose(1, 0, 2, 3, 4)
        both = jnp.concatenate(
            [both_in.reshape(2, rows_in, width), both[2 * rows_in :].reshape(2, ff_rows, width)],
            axis=1,
        )
        both = pick(both, group, 0).astype(f32) + send(pick(both, 1 - group, 0), "g").astype(f32)
        in_sums = both[:rows_in].reshape(2, 2, -1, width)
        sum_down = both[rows_in:]
        d_from_m, d_scale_m = whiten_back(d_normed_m, white_m, inv_m, scale_mlp)
        d_hidden = upstream + d_from_m
        all_da = gather_four((valid * d_hidden).astype(bf16))
        all_da, mlp_part = after(all_da, mlp_part)
        grad_out = dot_left_t(mixed, all_da).astype(bf16)
        output = hidden + valid * sum_four(mlp_part.astype(f32))
        output = moved(output.astype(bf16))[None]
        if aligned:
            sum_out = reduce_rows(out_pieces(grad_out), down_axes, forwards + ("g",))
        else:
            padded = lax.dynamic_update_slice_in_dim(
                jnp.zeros((width, width), bf16), grad_out, (2 * core + side) * head_cols, 0
            )
            sum_out = reduce_rows(padded, natural, forwards + ("g", "t", "c"))
        d_mixed = dot_right_t(all_da, w_out).astype(bf16).reshape(head_shape)
        d_query, d_key, d_value = attend_backward(query, key, value, log_sum, d_mixed, bias)
        d_packed = jnp.concatenate(
            [
                rotate(
                    d_query.astype(bf16).astype(f32).reshape(full_len, head_cols), cosine, -sine
                ).astype(bf16),
                rotate(
                    d_key.astype(bf16).astype(f32).reshape(full_len, head_cols), cosine, -sine
                ).astype(bf16),
                d_value.astype(bf16).reshape(full_len, head_cols),
            ],
            axis=1,
        )
        grad_qkv = dot_left_t(all_a, d_packed).astype(bf16)
        part = dot_right_t(d_packed, w_qkv).reshape(2, 2, span, width)
        from_core = send(part[:, 1].astype(bf16), "c")
        from_core, grad_qkv = after(from_core, grad_qkv)
        part = part[:, 0] + from_core.astype(f32)
        d_normed_a = part[0] + send(part[1].astype(bf16), "t").astype(f32)
        qkv_sums = jnp.concatenate(
            [
                reduce_rows(grad_qkv[:, :cut], natural, forwards + ("g",)),
                reduce_rows(grad_qkv[:, cut:], natural, backwards + ("g",)),
            ],
            axis=-1,
        )
        d_from_a, d_scale_a = whiten_back(d_normed_a, white_a, inv_a, scale_attn)
        grad_tokens = moved((d_hidden + d_from_a).astype(bf16))[None]

        raw_qkv = qkv_join(quad_back(qkv_sums.astype(bf16))).astype(f32)
        raw_in = in_join(quad_back(in_sums.astype(bf16))).astype(f32)
        sum_gain_a = jnp.sum(raw_qkv * qkv_weight.astype(f32), axis=1)
        sum_gain_m = jnp.sum(raw_in * in_weight.astype(f32), axis=1)
        sum_qkv = raw_qkv * gain_attn.astype(f32)[:, None]
        sum_in = raw_in * gain_mlp.astype(f32)[:, None]

        d_scale = jnp.concatenate([d_scale_a, d_scale_m], axis=1)
        d_scale = d_scale + send(d_scale, "c")
        d_scale = d_scale + send(d_scale, "t")
        d_both = join(d_scale[0], send(d_scale, "g")[0], group)
        rows_time = lax.dot_general(
            embed_rows,
            d_both,
            (((0,), (0,)), ((), ())),
            precision=lax.Precision.HIGHEST,
            preferred_element_type=f32,
        ).reshape((2,) * plane_bits + (-1, 2 * width))
        alive = list(backwards)
        for axis in backwards:
            at, mine = alive.index(axis), where[axis]
            rows_time = pick(rows_time, mine, at) + send(pick(rows_time, 1 - mine, at), axis)
            alive.remove(axis)
        return (
            output,
            grad_tokens,
            rows_time,
            sum_gain_a,
            sum_qkv,
            sum_out,
            sum_gain_m,
            sum_in,
            sum_down,
        )

    return per_device


def solution(mesh):
    seq_size, head_size = mesh.shape["seq"], mesh.shape["head"]
    own_mesh = Mesh(
        mesh.devices.reshape(seq_size // 2, 2, 2, head_size // 2),
        ("plane", "core", "group", "side"),
    )
    seq, head = ("plane", "core"), ("group", "side")
    rows, both, flat = P(seq + head, None), P(seq, head, None), P(seq + head)
    return jax.shard_map(
        build(seq_size, head_size),
        mesh=own_mesh,
        in_specs=(
            both,
            both,
            P(seq, None),
            P(seq),
            P(seq, None),
            rows,
            flat,
            rows,
            rows,
            flat,
            rows,
            rows,
        ),
        out_specs=(both, both, rows, flat, rows, rows, flat, rows, rows),
        check_vma=False,
    )
```

```python
import math

import jax
import jax.numpy as jnp
from jax import lax
from jax.experimental import pallas as pl
from jax.experimental.pallas import tpu as pltpu
from jax.sharding import Mesh
from jax.sharding import PartitionSpec as P

HEADS = 16
HD = 64

epsilon = 1e-05
f32 = jnp.float32
bf16 = jnp.bfloat16


def dot(left, right):
    return jnp.dot(left, right, preferred_element_type=f32)


def dot_right_t(left, right):
    return lax.dot_general(left, right, (((1,), (1,)), ((), ())), preferred_element_type=f32)


def dot_left_t(left, right):
    return lax.dot_general(left, right, (((0,), (0,)), ((), ())), preferred_element_type=f32)


def whiten(field):
    centre = jnp.mean(field, axis=-1, keepdims=True)
    shifted = field - centre
    variance = jnp.mean(shifted * shifted, axis=-1, keepdims=True)
    inv_std = lax.rsqrt(variance + epsilon)
    return shifted * inv_std, inv_std


def whiten_back(d_normed, whitened, inv_std, scale_vec):
    d_scale = jnp.sum(d_normed * whitened, axis=0, keepdims=True)
    d_white = d_normed * scale_vec
    d_input = inv_std * (
        d_white
        - jnp.mean(d_white, axis=-1, keepdims=True)
        - whitened * jnp.mean(d_white * whitened, axis=-1, keepdims=True)
    )
    return d_input, d_scale


PAIR = 2 * HD


def rope_tables(positions):
    half_dim = HD // 2
    inverse_freq = jnp.power(10000.0, -jnp.arange(half_dim, dtype=f32) * 2.0 / HD)
    angles = positions.astype(f32)[:, None] * jnp.tile(inverse_freq, PAIR // half_dim)[None, :]
    return jnp.cos(angles), jnp.sin(angles)


def turn(field, cosine, sine, sign):
    lane = lax.broadcasted_iota(jnp.int32, field.shape, 1)
    first = lane % HD < HD // 2
    other = jnp.where(
        first, -pltpu.roll(field, PAIR - HD // 2, 1), pltpu.roll(field, HD // 2, 1)
    )
    return field * cosine + other * sine * sign


def only(field, head):
    lane = lax.broadcasted_iota(jnp.int32, field.shape, 1)
    return jnp.where(lane // HD == head, field, jnp.zeros_like(field))


def attend_forward_kernel(
    q_in, k_in, v_in, cosine, sine, usable, q_out, k_out, v_out, mixed, logs
):
    block = min(256, q_in.shape[0])
    scale = 1.0 / math.sqrt(HD)
    q_out[...] = turn(q_in[...], cosine[...], sine[...], 1.0).astype(bf16)
    k_out[...] = turn(k_in[...], cosine[...], sine[...], 1.0).astype(bf16)
    v_out[...] = v_in[...].astype(bf16)
    fits = usable[...] > 0

    def step(at, _):
        rows = pl.ds(pl.multiple_of(at * block, block), block)
        query, key, value = q_out[rows, :], k_out[...], v_out[...]
        total = jnp.zeros((block, PAIR), f32)
        log = []
        for head in range(2):
            scores = dot_right_t(only(query, head), key) * scale
            scores = jnp.where(fits, scores, -1e30)
            row_max = jnp.max(scores, axis=-1, keepdims=True)
            weights = jnp.exp(scores - row_max)
            row_sum = jnp.sum(weights, axis=-1, keepdims=True)
            low = (weights * (1.0 / row_sum)).astype(bf16)
            total = total + dot(low, only(value, head))
            log.append(jnp.broadcast_to(row_max + jnp.log(row_sum), (block, PAIR)))
        lane = lax.broadcasted_iota(jnp.int32, (block, PAIR), 1)
        mixed[rows, :] = total.astype(bf16)
        logs[rows, :] = jnp.where(lane < HD, log[0], log[1])
        return 0

    lax.fori_loop(0, q_in.shape[0] // block, step, 0)


def attend_backward_kernel(
    q_in, k_in, v_in, logs, d_mixed, cosine, sine, usable, dq_out, dk_out, dv_out, d_key, d_value
):
    block = min(256, q_in.shape[0])
    scale = 1.0 / math.sqrt(HD)
    fits = usable[...] > 0
    d_key[...] = jnp.zeros_like(d_key)
    d_value[...] = jnp.zeros_like(d_value)

    def step(at, _):
        rows = pl.ds(pl.multiple_of(at * block, block), block)
        query, key, value, d_block = q_in[rows, :], k_in[...], v_in[...], d_mixed[rows, :]
        log = logs[rows, :]
        d_query = jnp.zeros((block, PAIR), f32)
        for head in range(2):
            q_head, d_head = only(query, head), only(d_block, head)
            scores = dot_right_t(q_head, key) * scale
            scores = jnp.where(fits, scores, -1e30)
            probs = jnp.exp(scores - log[:, head * HD : head * HD + 1])
            d_value[...] += dot_left_t(probs.astype(bf16), d_head)
            d_probs = dot_right_t(d_head, value)
            row_dot = jnp.sum(d_probs * probs, axis=-1, keepdims=True)
            d_scores = (probs * (d_probs - row_dot)).astype(bf16)
            d_query = d_query + dot(d_scores, only(key, head))
            d_key[...] += dot_left_t(d_scores, q_head)
        d_query = (d_query * scale).astype(bf16).astype(f32)
        dq_out[rows, :] = turn(d_query, cosine[rows, :], sine[rows, :], -1.0).astype(bf16)
        return 0

    lax.fori_loop(0, q_in.shape[0] // block, step, 0)
    turned = (d_key[...] * scale).astype(bf16).astype(f32)
    dk_out[...] = turn(turned, cosine[...], sine[...], -1.0).astype(bf16)
    dv_out[...] = d_value[...].astype(bf16)


def attend_forward(packed, cosine, sine, usable):
    length, pairs = packed.shape[0], packed.shape[1] // (3 * PAIR)
    column = lambda first: pl.BlockSpec((length, PAIR), lambda i: (0, first + i))
    fixed = pl.BlockSpec((length, PAIR), lambda i: (0, 0))
    row = pl.BlockSpec((1, length), lambda i: (0, 0))
    low = jax.ShapeDtypeStruct((length, pairs * PAIR), bf16)
    return pl.pallas_call(
        attend_forward_kernel,
        grid=(pairs,),
        in_specs=[column(0), column(pairs), column(2 * pairs), fixed, fixed, row],
        out_specs=[column(0)] * 5,
        out_shape=[low] * 4 + [jax.ShapeDtypeStruct((length, pairs * PAIR), f32)],
        compiler_params=pltpu.CompilerParams(vmem_limit_bytes=40 << 20),
        cost_estimate=pl.CostEstimate(
            flops=pairs * 16 * length * length * PAIR,
            bytes_accessed=length * pairs * PAIR * 24,
            transcendentals=pairs * 2 * length * length,
        ),
    )(packed, packed, packed, cosine, sine, usable)


def attend_backward(query, key, value, logs, d_mixed, cosine, sine, usable, pair):
    length = query.shape[0]
    column = pl.BlockSpec((length, PAIR), lambda i: (0, pair))
    fixed = pl.BlockSpec((length, PAIR), lambda i: (0, 0))
    row = pl.BlockSpec((1, length), lambda i: (0, 0))
    low = jax.ShapeDtypeStruct((length, PAIR), bf16)
    return pl.pallas_call(
        attend_backward_kernel,
        grid=(1,),
        in_specs=[column] * 5 + [fixed, fixed, row],
        out_specs=[fixed] * 3,
        out_shape=[low] * 3,
        scratch_shapes=[pltpu.VMEM((length, PAIR), f32)] * 2,
        compiler_params=pltpu.CompilerParams(vmem_limit_bytes=40 << 20),
        cost_estimate=pl.CostEstimate(
            flops=40 * length * length * PAIR,
            bytes_accessed=length * PAIR * 24,
            transcendentals=2 * length * length,
        ),
    )(query, key, value, logs, d_mixed, cosine, sine, usable)


def build(seq_size, head_size):
    plane_bits = (seq_size // 2).bit_length() - 1
    planes = seq_size // 2
    assert planes == 1 << plane_bits and seq_size >= 2 and head_size == 4

    def swap(x, axis, mask, size):
        return lax.ppermute(x, axis, [(i, i ^ mask) for i in range(size)])

    def pick(x, index, axis):
        return lax.dynamic_index_in_dim(x, index, axis, keepdims=False)

    def join(own, other, bit, axis=0):
        return jnp.where(
            bit == 0, jnp.stack([own, other], axis=axis), jnp.stack([other, own], axis=axis)
        )

    def per_device(
        tokens,
        cotangent,
        time_embed,
        lengths,
        key_mask,
        time_weight,
        gain_attn,
        qkv_weight,
        out_weight,
        gain_mlp,
        in_weight,
        down_weight,
    ):
        core, plane = lax.axis_index("core"), lax.axis_index("plane")
        group, side = lax.axis_index("group"), lax.axis_index("side")
        stays = core == group
        _, span, width = tokens.shape
        full_len = span * head_size
        hidden_cols = in_weight.shape[1]
        head_cols, ff_cols = width // 4, hidden_cols // 4
        forwards = tuple(range(plane_bits))
        backwards = tuple(reversed(forwards))
        where = {"c": core, "g": group, "t": side}
        where.update({bit: (plane >> bit) & 1 for bit in range(plane_bits)})
        natural = list(backwards) + ["c", "g", "t"]

        def send(x, axis):
            if axis in ("c", "g", "t"):
                name = {"c": "core", "g": "group", "t": "side"}[axis]
                return swap(x, name, 1, 2)
            return swap(x, "plane", 1 << axis, planes)

        def moved(x):
            return jnp.where(stays, x, lax.ppermute(x, ("core", "group"), [(1, 2), (2, 1)]))

        def after(x, first):
            return lax.optimization_barrier((x, first))

        def gather(x, labels, axes):
            for axis in axes:
                x = join(x, send(x, axis), where[axis])
                labels = [axis] + labels
            return x, labels

        def in_order(x, labels):
            wanted = [axis for axis in natural if axis in labels]
            perm = [labels.index(axis) for axis in wanted]
            x = x.transpose(perm + list(range(len(perm), x.ndim)))
            return x.reshape(-1, x.shape[-1])

        def exchange(parts, axis):
            mine = where[axis]
            return join(pick(parts, mine, 0), send(pick(parts, 1 - mine, 0), axis), mine)

        def reduce_rows(x, labels, axes):
            labels = [axis for axis in natural if axis in labels]
            y = x.astype(bf16).reshape((2,) * len(labels) + (-1, x.shape[-1]))
            for step, axis in enumerate(axes):
                at, mine = labels.index(axis), where[axis]
                other = send(pick(y, 1 - mine, at), axis)
                y = pick(y, mine, at).astype(f32) + other.astype(f32)
                if step + 1 < len(axes):
                    y = y.astype(bf16)
                labels.remove(axis)
            return y

        chunk = out_weight.shape[0] * head_size
        aligned = (chunk % HD == 0) and (width // (2 * chunk)) % 2 == 0

        def qkv_split(w):
            rows = w.shape[0]
            if aligned:
                w = w.reshape(rows, 3, 2, -1, 2, chunk).transpose(4, 2, 0, 1, 3, 5)
            else:
                w = w.reshape(rows, 3, 2, 2, head_cols).transpose(2, 3, 0, 1, 4)
            return w.reshape(2, 2, rows, 3 * head_cols)

        def qkv_join(w):
            rows = w.shape[2]
            if aligned:
                w = w.reshape(2, 2, rows, 3, -1, chunk).transpose(2, 3, 1, 4, 0, 5)
            else:
                w = w.reshape(2, 2, rows, 3, head_cols).transpose(2, 3, 0, 1, 4)
            return w.reshape(rows, 3 * width)

        ff_rows = down_weight.shape[0]

        def in_split(w):
            rows = w.shape[0]
            w = w.reshape(rows, planes, 2, 2, 2, ff_rows).transpose(2, 4, 0, 1, 3, 5)
            return w.reshape(2, 2, rows, ff_cols)

        def in_join(w):
            rows = w.shape[2]
            w = w.reshape(2, 2, rows, planes, 2, ff_rows).transpose(2, 3, 0, 4, 1, 5)
            return w.reshape(rows, hidden_cols)

        def quad(parts):
            x = exchange(parts, "c")
            return exchange(x.transpose(1, 0, 2, 3), "t"), x

        def quad_back(x):
            x = exchange(x, "c")
            x = exchange(x.transpose(1, 0, 2, 3), "t")
            return x.transpose(1, 0, 2, 3)

        aux = jnp.concatenate(
            [
                key_mask.astype(f32),
                time_embed.astype(f32),
                jnp.broadcast_to(lengths.astype(f32)[:, None], (1, 128)),
            ],
            axis=1,
        )
        aux_other = send(aux, "c")
        aux_both = join(aux[0], aux_other[0], core)
        embed_both = aux_both[:, full_len : full_len + time_embed.shape[1]]
        aux_mine = pick(aux_both, group, 0)
        length = aux_mine[full_len + time_embed.shape[1]].astype(jnp.int32)
        usable = jnp.logical_and(
            aux_mine[:full_len] > 0, jnp.arange(full_len, dtype=jnp.int32) < length
        )

        piece = out_weight.shape[0]

        def out_heads(x):
            x = x.reshape(2, -1, piece, width)
            x = exchange(x, "t")
            return x.transpose(1, 0, 2, 3).reshape(head_cols, width)

        def out_pieces(x):
            x = x.reshape(-1, 2, piece, width).transpose(1, 0, 2, 3)
            return exchange(x, "t").reshape(head_cols, width)

        qkv_scaled = (qkv_weight.astype(f32) * gain_attn.astype(f32)[:, None]).astype(bf16)
        in_scaled = (in_weight.astype(f32) * gain_mlp.astype(f32)[:, None]).astype(bf16)
        qkv_quad, _ = quad(qkv_split(qkv_scaled))
        time_rows, qkv_quad = after(time_weight, qkv_quad)
        w_qkv, labels = gather(qkv_quad, ["t", "c"], ["g"])
        later, w_qkv = after(cotangent[0], w_qkv)
        out_later, w_qkv = after(out_weight, w_qkv)
        cut = 3 * head_cols // 2
        w_qkv = jnp.concatenate(
            [
                in_order(*gather(w_qkv[..., :cut], labels, forwards)),
                in_order(*gather(w_qkv[..., cut:], labels, backwards)),
            ],
            axis=1,
        )
        in_quad, _ = quad(in_split(in_scaled))
        rows_in = 4 * in_weight.shape[0]
        packs = jnp.concatenate([in_quad.reshape(rows_in, width), down_weight])
        packs = lax.all_gather(packs, ("plane", "group"), axis=0)
        w_in = packs[:, :rows_in].reshape(planes, 2, 2, 2, -1, width)
        w_in = w_in.transpose(0, 3, 1, 2, 4, 5).reshape(width, ff_cols)
        w_down = packs[:, rows_in : rows_in + ff_rows].reshape(ff_cols, width)
        if aligned:
            w_out = in_order(*gather(out_later, [], ("g",) + forwards))
            w_out = out_heads(w_out)
        else:
            w_out, labels = gather(out_weight, [], ("c", "t", "g") + forwards)
            w_out = lax.dynamic_slice_in_dim(
                in_order(w_out, labels), (2 * core + side) * head_cols, head_cols, 0
            )

        t_rows, labels = gather(time_rows, [], forwards[:1])
        t_rows = in_order(*gather(t_rows, labels, forwards[1:]))
        embed_rows = pick(
            pick(embed_both.reshape(2, planes, 2, head_size, -1), core, 2), 2 * group + side, 2
        ).reshape(2, -1)
        part = jnp.dot(
            embed_rows, t_rows.astype(f32), precision=lax.Precision.HIGHEST
        )
        part_mine = pick(part, group, 0) + send(pick(part, 1 - group, 0), "g")
        part_mine = part_mine + send(part_mine, "t")
        scales = 1.0 + (part_mine + send(part_mine, "c"))
        scale_attn, scale_mlp = scales[None, :width], scales[None, width:]

        blocks = (
            side + 2 * core,
            side + 2 - 2 * core,
            1 - side + 2 * core,
            1 - side + 2 - 2 * core,
        )
        steps = jnp.arange(span, dtype=jnp.int32)
        valid = (blocks[0] * span + steps < length).astype(f32)[:, None]
        cosine, sine = rope_tables(jnp.concatenate([block * span + steps for block in blocks]))
        usable_blocks = usable.reshape(head_size, span)
        usable_row = jnp.concatenate([pick(usable_blocks, block, 0) for block in blocks])
        usable_row = usable_row.astype(f32)[None, :]

        def gather_four(x):
            across = send(x, "t")
            return jnp.concatenate([x, send(x, "c"), across, send(across, "c")])

        def sum_four(x):
            x = x.reshape(2, 2, span, width)
            x = x[:, 0] + send(x[:, 1].astype(bf16), "c").astype(f32)
            return x[0] + send(x[1].astype(bf16), "t").astype(f32)

        inputs = moved(tokens[0]).astype(f32)
        w_qkv, upstream = after(w_qkv, moved(later))
        upstream = upstream.astype(f32)
        own_d = (valid * upstream).astype(bf16)
        across_d, core_d = send(own_d, "t"), send(own_d, "c")
        white_a, inv_a = whiten(inputs)
        all_a = gather_four((white_a * scale_attn).astype(bf16))
        packed = dot(all_a, w_qkv)
        across_d, core_d, packed = lax.optimization_barrier((across_d, core_d, packed))
        all_d = jnp.concatenate([own_d, core_d, across_d, send(across_d, "c")])
        w_out, all_d = after(w_out, all_d)
        query, key, value, mixed, logs = attend_forward(packed, cosine, sine, usable_row)

        hidden = inputs + valid * sum_four(dot(mixed, w_out))
        white_m, inv_m = whiten(hidden)
        all_m = gather_four((white_m * scale_mlp).astype(bf16))
        upper = dot(all_m, w_in)
        phi = 0.5 * (1.0 + lax.erf(upper / math.sqrt(2.0)))
        activation = (upper * phi).astype(bf16)
        slope = phi + upper * jnp.exp(-0.5 * upper * upper) / math.sqrt(2.0 * math.pi)
        activation, slope = lax.optimization_barrier((activation, slope))
        mlp_part = dot(activation, w_down).astype(bf16)

        d_upper = (dot_right_t(all_d, w_down) * slope).astype(bf16)
        down_axes = [axis for axis in natural if axis not in ("c", "t")]
        grad_down = dot_left_t(activation, all_d).astype(bf16).reshape(planes, 2 * ff_rows, width)
        d_normed_m = sum_four(dot_right_t(d_upper, w_in))
        grad_in = dot_left_t(all_m, d_upper).astype(bf16).reshape(planes, 2 * rows_in, width)
        sum_d = lax.psum_scatter(grad_down, "plane", scatter_dimension=0, tiled=True)[0]
        sum_i = lax.psum_scatter(grad_in, "plane", scatter_dimension=0, tiled=True)[0]
        sum_i = sum_i.reshape(2, 2, 2, -1, width).transpose(1, 0, 2, 3, 4)
        sum_i = sum_i.reshape(2, rows_in, width)
        sum_d = sum_d.reshape(2, ff_rows, width)

        def over_group(x):
            return pick(x, group, 0).astype(f32) + send(pick(x, 1 - group, 0), "g").astype(f32)

        sum_down = over_group(sum_d)
        in_sums = over_group(sum_i).reshape(2, 2, -1, width)
        d_from_m, d_scale_m = whiten_back(d_normed_m, white_m, inv_m, scale_mlp)
        d_hidden = upstream + d_from_m
        all_da = gather_four((valid * d_hidden).astype(bf16))
        all_da, mlp_part = after(all_da, mlp_part)
        grad_out = dot_left_t(mixed, all_da).astype(bf16)
        mlp_part = mlp_part.reshape(2, 2, span, width)
        out_core = send(mlp_part[:, 1], "c")
        if aligned:
            sum_out = reduce_rows(out_pieces(grad_out), down_axes, forwards + ("g",))
        else:
            padded = lax.dynamic_update_slice_in_dim(
                jnp.zeros((width, width), bf16), grad_out, (2 * core + side) * head_cols, 0
            )
            sum_out = reduce_rows(padded, natural, forwards + ("g", "t", "c"))
        d_mixed = dot_right_t(all_da, w_out).astype(bf16)
        halves = []
        for pair in range(head_cols // PAIR):
            halves.append(
                attend_backward(query, key, value, logs, d_mixed, cosine, sine, usable_row, pair)
            )
            if pair == 0:
                halves[0], d_mixed, out_core, sum_down = lax.optimization_barrier(
                    (halves[0], d_mixed, out_core, sum_down)
                )
                mlp_sum = mlp_part[:, 0].astype(f32) + out_core.astype(f32)
                output = mlp_sum[0] + send(mlp_sum[1].astype(bf16), "t").astype(f32)
                output = (hidden + valid * output).astype(bf16)
        d_packed = jnp.concatenate([half[k] for k in range(3) for half in halves], axis=1)
        d_packed, output, sum_out, in_sums = lax.optimization_barrier(
            (d_packed, output, sum_out, in_sums)
        )
        output = moved(output)[None]
        grad_qkv = dot_left_t(all_a, d_packed).astype(bf16)
        part = dot_right_t(d_packed, w_qkv).reshape(2, 2, span, width)
        from_core = send(part[:, 1].astype(bf16), "c")
        from_core, grad_qkv = after(from_core, grad_qkv)
        part = part[:, 0] + from_core.astype(f32)
        d_normed_a = part[0] + send(part[1].astype(bf16), "t").astype(f32)
        qkv_sums = jnp.concatenate(
            [
                reduce_rows(grad_qkv[:, :cut], natural, forwards + ("g",)),
                reduce_rows(grad_qkv[:, cut:], natural, backwards + ("g",)),
            ],
            axis=-1,
        )
        d_from_a, d_scale_a = whiten_back(d_normed_a, white_a, inv_a, scale_attn)
        grad_tokens = moved((d_hidden + d_from_a).astype(bf16))[None]

        raw_qkv = qkv_join(quad_back(qkv_sums.astype(bf16))).astype(f32)
        raw_in = in_join(quad_back(in_sums.astype(bf16))).astype(f32)
        sum_gain_a = jnp.sum(raw_qkv * qkv_weight.astype(f32), axis=1)
        sum_gain_m = jnp.sum(raw_in * in_weight.astype(f32), axis=1)
        sum_qkv = raw_qkv * gain_attn.astype(f32)[:, None]
        sum_in = raw_in * gain_mlp.astype(f32)[:, None]

        d_scale = jnp.concatenate([d_scale_a, d_scale_m], axis=1)
        d_scale = d_scale + send(d_scale, "c")
        d_scale = d_scale + send(d_scale, "t")
        d_both = join(d_scale[0], send(d_scale, "g")[0], group)
        rows_time = lax.dot_general(
            embed_rows,
            d_both,
            (((0,), (0,)), ((), ())),
            precision=lax.Precision.HIGHEST,
            preferred_element_type=f32,
        ).reshape((2,) * plane_bits + (-1, 2 * width))
        alive = list(backwards)
        for axis in backwards:
            at, mine = alive.index(axis), where[axis]
            rows_time = pick(rows_time, mine, at) + send(pick(rows_time, 1 - mine, at), axis)
            alive.remove(axis)
        return (
            output,
            grad_tokens,
            rows_time,
            sum_gain_a,
            sum_qkv,
            sum_out,
            sum_gain_m,
            sum_in,
            sum_down,
        )

    return per_device


def solution(mesh):
    seq_size, head_size = mesh.shape["seq"], mesh.shape["head"]
    own_mesh = Mesh(
        mesh.devices.reshape(seq_size // 2, 2, 2, head_size // 2),
        ("plane", "core", "group", "side"),
    )
    seq, head = ("plane", "core"), ("group", "side")
    rows, both, flat = P(seq + head, None), P(seq, head, None), P(seq + head)
    return jax.shard_map(
        build(seq_size, head_size),
        mesh=own_mesh,
        in_specs=(
            both,
            both,
            P(seq, None),
            P(seq),
            P(seq, None),
            rows,
            flat,
            rows,
            rows,
            flat,
            rows,
            rows,
        ),
        out_specs=(both, both, rows, flat, rows, rows, flat, rows, rows),
        check_vma=False,
    )
```
